768 devices in a mesh: seq: 64 (over y, x, core), head: 12 (over z).
Axes of the slice: x: 4, y: 8, z: 12, core: 2. Of those that a mesh axis runs over, the one named last changes fastest.
Arguments:
- queries: float32 [32768, 3072], P('seq', 'head'), may hold values from -6 to 6
- keys: float32 [32768, 3072], P('seq', 'head'), may hold values from -6 to 6
- values: float32 [32768, 3072], P('seq', 'head'), may hold values from -60 to 60
- cotangent: float32 [32768, 3072], P('seq', 'head'), may hold values from -6 to 6
- gain: float32 [3072], P('head'), may hold values from 0.1 to 1.9
Outputs:
- grad_queries: float32 [32768, 3072], P('seq', 'head')
- grad_keys: float32 [32768, 3072], P('seq', 'head')
- grad_values: float32 [32768, 3072], P('seq', 'head')
The draws below stay inside these ranges and needn't reach their ends.
All inputs are finite; a program needn't handle non-finite values.
Results may differ from the reference program's by a relative error of at most 0.0001.
Values sent between devices are 32-bit elements; how exact they have to be, the bound alone decides.
A program may use at most 64 MiB of HBM per device.

```python
import math
import jax
import jax.numpy as jnp
from jax import lax

HD = 128
HEADS = 24
D = 3072
TOKENS = 32768


def draw_values(key, part):
    key_spread = jax.random.fold_in(key, 11)
    key_noise = jax.random.fold_in(key, 12)
    head_index = jnp.arange(HEADS).astype(jnp.float32)
    rising = 3.0 ** (head_index / (HEADS - 1))
    spreads = jnp.exp(jax.random.uniform(key_spread, (HEADS,), minval=0.0, maxval=math.log(3.5)))
    head_scale = jnp.repeat(rising * spreads, HD)
    noise_field = jnp.clip(jax.random.normal(key_noise, (TOKENS, D)), -5.0, 5.0)
    return (noise_field * head_scale[None, :]).astype(jnp.float32)


def block_scale(rng, dims, shards, least, largest):
    def one(position, blocks):
        steps = jax.random.uniform(jax.random.fold_in(jax.random.fold_in(rng, 6), position), (blocks,), jnp.float32, least / len(shards), largest / len(shards))
        return jnp.repeat(jnp.exp(steps), dims[position] // blocks).reshape((-1,) + (1,) * (len(dims) - position - 1))

    factor_of = one(*shards[0])
    for cut in shards[1:]:
        factor_of = factor_of * one(*cut)
    return factor_of


def noise(key, dims, scale, reach, shards=(), dtype=jnp.bfloat16):
    result = jax.random.normal(key, dims, jnp.float32) * scale
    if len(shards) > 0:
        result = block_scale(key, dims, shards, -0.22, 0.18) * result
    return jnp.clip(result, min=-reach, max=reach).astype(dtype)


def setup_inputs(seed: int = 0) -> dict:
    streams_of = jax.random.split(jax.random.key(seed), 6)
    return {
        "queries": noise(streams_of[0], (TOKENS, D), 1.0, 6.0, ((0, 64), (1, 12)), jnp.float32),
        "keys": noise(streams_of[1], (TOKENS, D), 1.0, 6.0, ((0, 64), (1, 12)), jnp.float32),
        "values": draw_values(jax.random.fold_in(streams_of[5], 71), 0),
        "cotangent": noise(streams_of[3], (TOKENS, D), 1.0, 6.0, ((0, 64), (1, 12)), jnp.float32),
        "gain": jnp.clip(1.0 + 0.18 * jax.random.normal(streams_of[4], (D,), jnp.float32), 0.1, 1.9),
    }


def product(form, left, right):
    return jnp.einsum(form, left, right, precision=lax.Precision.HIGHEST)

def to_blocks(array, block):
    return array.reshape(TOKENS // block, block, HEADS, HD).transpose(0, 2, 1, 3)

def from_blocks(array):
    return array.transpose(0, 2, 1, 3).reshape(TOKENS, HEADS * HD)

def reference(queries, keys, values, cotangent, gain):
    block = min(512, TOKENS)
    query_blocks = to_blocks(queries, block)
    key_blocks = to_blocks(keys, block)
    value_blocks = to_blocks(values, block)
    causal = (jnp.arange(block)[:, None] >= jnp.arange(block)[None, :]).astype(jnp.float32)

    def forward_step(state, inputs):
        query_now, key_now, value_now = inputs
        scores = product('htd,hsd->hts', query_now, key_now) * causal
        attended = product('hts,hse->hte', scores, value_now) + product('htd,hde->hte', query_now, state)
        new_state = state + product('hsd,hse->hde', key_now, value_now)
        return (new_state, (attended, state))
    start_state = jnp.zeros((HEADS, HD, HD), jnp.float32)
    unused_state, (attended_blocks, state_before) = lax.scan(forward_step, start_state, (query_blocks, key_blocks, value_blocks))
    attended_rows = from_blocks(attended_blocks)
    scaled_cot = gain[None, :] * cotangent
    inverse = lax.rsqrt(lax.optimization_barrier(jnp.mean(attended_rows * attended_rows, axis=1)) + 1e-06)
    cross = lax.optimization_barrier(jnp.mean(scaled_cot * attended_rows, axis=1))
    grad_rows = inverse[:, None] * scaled_cot - attended_rows * (inverse * inverse * inverse * cross)[:, None]
    grad_blocks = to_blocks(grad_rows, block)

    def backward_step(state_after, inputs):
        query_now, key_now, value_now, grad_now, before_now = inputs
        scores = product('htd,hsd->hts', query_now, key_now) * causal
        mixing = product('hte,hse->hts', grad_now, value_now) * causal
        grad_q = product('hts,hsd->htd', mixing, key_now) + product('hde,hte->htd', before_now, grad_now)
        grad_k = product('hts,htd->hsd', mixing, query_now) + product('hde,hse->hsd', state_after, value_now)
        grad_v = product('hts,hte->hse', scores, grad_now) + product('hde,hsd->hse', state_after, key_now)
        new_after = state_after + product('htd,hte->hde', query_now, grad_now)
        return (new_after, (grad_q, grad_k, grad_v))
    unused_after, (grad_q, grad_k, grad_v) = lax.scan(backward_step, start_state, (query_blocks, key_blocks, value_blocks, grad_blocks, state_before), reverse=True)
    return (from_blocks(grad_q), from_blocks(grad_k), from_blocks(grad_v))
```

```python
import functools

import jax
import jax.numpy as jnp
from jax import lax
from jax.experimental import pallas as pl
from jax.experimental.pallas import tpu as pltpu
from jax.sharding import PartitionSpec as P

HD = 128
ROW = 8
CHUNK = 256
EPS = 1e-06
MESH = pl.DeviceIdType.MESH
F32 = jnp.float32
BF16 = jnp.bfloat16


def split(x):
    high = x.astype(BF16)
    return high, (x - high.astype(F32)).astype(BF16)


def dot3(left, right, dims):
    def one(a, b):
        return lax.dot_general(a, b, (dims, ((), ())), preferred_element_type=F32)

    (lh, ll), (rh, rl) = left, right
    return one(lh, rh) + (one(lh, rl) + one(ll, rh))


NN = ((1,), (0,))
NT = ((1,), (1,))
TN = ((0,), (0,))


def body(
    n_seq,
    n_head,
    q_hbm,
    k_hbm,
    v_hbm,
    cot_hbm,
    gain_ref,
    gq_hbm,
    gk_hbm,
    gv_hbm,
    q_s,
    k_s,
    v_s,
    sc_s,
    att_s,
    gq_s,
    gk_s,
    gv_s,
    qh,
    ql,
    kh,
    kl,
    vh,
    vl,
    gh,
    gl,
    sco_h,
    sco_l,
    bd_h,
    bd_l,
    own,
    row_in,
    col_in,
    row_out,
    state,
    norm_own,
    norm_in,
    in_sem,
    out_sem,
    send_sem,
    recv_sem,
):
    n_y = n_seq // ROW
    tokens, width = q_s.shape
    heads = width // HD
    chunks = tokens // CHUNK
    part = heads * HD // ROW
    s = lax.axis_index("seq")
    h = lax.axis_index("head")
    j = lax.rem(s, ROW)
    y = lax.div(s, ROW)

    def row_peer(k):
        return (y * ROW + lax.rem(j + k, ROW), h)

    def col_peer(m):
        return (lax.rem(y + m, n_y) * ROW + j, h)

    def head_peer(m):
        return (s, lax.rem(h + m, n_head))

    loads = [
        pltpu.make_async_copy(src, dst, in_sem.at[i])
        for i, (src, dst) in enumerate(
            [(k_hbm, k_s), (v_hbm, v_s), (q_hbm, q_s), (cot_hbm, sc_s)]
        )
    ]
    for load in loads:
        load.start()
    barrier = pltpu.get_barrier_semaphore()
    peers = (
        [row_peer(k) for k in range(1, ROW)]
        + [col_peer(m) for m in range(1, n_y)]
        + [head_peer(m) for m in range(1, n_head)]
    )
    for peer in peers:
        pl.semaphore_signal(barrier, inc=1, device_id=peer, device_id_type=MESH)

    def send(src, dst, stage, peer):
        pltpu.make_async_remote_copy(
            src_ref=src,
            dst_ref=dst,
            send_sem=send_sem.at[stage],
            recv_sem=recv_sem.at[stage],
            device_id=peer,
            device_id_type=MESH,
        ).start()

    def wait_in(ref, stage):
        pltpu.make_async_remote_copy(
            src_ref=ref,
            dst_ref=ref,
            send_sem=send_sem.at[stage],
            recv_sem=recv_sem.at[stage],
            device_id=row_peer(1),
            device_id_type=MESH,
        ).wait_recv()

    def wait_out(ref, stage):
        pltpu.make_async_remote_copy(
            src_ref=ref,
            dst_ref=ref,
            send_sem=send_sem.at[stage],
            recv_sem=recv_sem.at[stage],
            device_id=row_peer(1),
            device_id_type=MESH,
        ).wait_send()

    def weight(cond):
        return jnp.where(cond, 1.0, 0.0).astype(F32)

    def scan_row(scan):
        for k in range(1, ROW):
            there = lax.rem(j + k, ROW)
            send(
                own.at[scan, pl.ds(pl.multiple_of(there * part, part), part)],
                row_in.at[scan, k - 1],
                3 * scan,
                row_peer(k),
            )

    def scan_col(scan):
        wait_in(row_in.at[scan], 3 * scan)
        total = own[scan, pl.ds(pl.multiple_of(j * part, part), part)]
        for k in range(1, ROW):
            total = total + row_in[scan, k - 1]
        col_in[scan, n_y - 1] = total
        for m in range(1, n_y):
            send(
                col_in.at[scan, n_y - 1],
                col_in.at[scan, m - 1],
                3 * scan + 1,
                col_peer(m),
            )

    def scan_back(scan):
        if n_y > 1:
            wait_in(col_in.at[scan, pl.ds(0, n_y - 1)], 3 * scan + 1)
        base = jnp.zeros((part, HD), F32)
        for m in range(1, n_y):
            inside = (y < m) if scan else (y >= m)
            base = base + weight(inside) * col_in[scan, m - 1]
        mine = own[scan, pl.ds(pl.multiple_of(j * part, part), part)]
        for k in range(ROW):
            there = lax.rem(j + k, ROW)
            value = base
            for r in range(ROW):
                source = lax.rem(j - r + ROW, ROW)
                inside = (source > there) if scan else (source < there)
                piece = mine if r == 0 else row_in[scan, r - 1]
                if r != k or k == 0:
                    pass
                value = value + weight(inside) * piece
            if k == 0:
                state[scan, pl.ds(pl.multiple_of(j * part, part), part)] = value
            else:
                row_out[scan, k - 1] = value
                send(
                    row_out.at[scan, k - 1],
                    state.at[scan, pl.ds(pl.multiple_of(j * part, part), part)],
                    3 * scan + 2,
                    row_peer(k),
                )

    def scan_end(scan):
        wait_in(state.at[scan, pl.ds(0, (ROW - 1) * part)], 3 * scan + 2)

    def cols(head):
        return slice(head * HD, (head + 1) * HD)

    def rows(chunk):
        return slice(chunk * CHUNK, (chunk + 1) * CHUNK)

    def diagonal(full):
        return jnp.concatenate([full[cols(i), cols(i)] for i in range(heads)], axis=0)

    def put_block_diagonal(slot, stacked):
        high, low = split(stacked)
        for i in range(heads):
            bd_h[slot, cols(i), cols(i)] = high[cols(i)]
            bd_l[slot, cols(i), cols(i)] = low[cols(i)]

    def pair(high, low, *index):
        return high[index], low[index]

    bd_h[...] = jnp.zeros_like(bd_h)
    bd_l[...] = jnp.zeros_like(bd_l)
    lower = lax.broadcasted_iota(jnp.int32, (CHUNK, CHUNK), 0) >= lax.broadcasted_iota(
        jnp.int32, (CHUNK, CHUNK), 1
    )

    loads[0].wait()
    kh[...], kl[...] = split(k_s[...])
    loads[1].wait()
    vh[...], vl[...] = split(v_s[...])
    total = jnp.zeros((heads * HD, HD), F32)
    for c in range(chunks):
        here = diagonal(dot3(pair(kh, kl, rows(c)), pair(vh, vl, rows(c)), TN))
        total = total + here
        if c + 1 < chunks:
            put_block_diagonal(c, total)
    own[0] = total
    pl.semaphore_wait(barrier, len(peers))
    scan_row(0)

    loads[2].wait()
    qh[...], ql[...] = split(q_s[...])
    for c in range(chunks):
        for i in range(heads):
            scores = dot3(
                pair(qh, ql, rows(c), cols(i)), pair(kh, kl, rows(c), cols(i)), NT
            )
            sco_h[c, i], sco_l[c, i] = split(jnp.where(lower, scores, 0.0))
    loads[3].wait()
    sc_s[...] = sc_s[...] * gain_ref[...]
    scan_col(0)
    for c in range(chunks):
        for i in range(heads):
            inner = dot3(pair(sco_h, sco_l, c, i), pair(vh, vl, rows(c), cols(i)), NN)
            att_s[rows(c), cols(i)] = inner
        if c > 0:
            att_s[rows(c)] += dot3(
                pair(qh, ql, rows(c)), pair(bd_h, bd_l, c - 1), NN
            )
    scan_back(0)
    scan_end(0)

    put_block_diagonal(chunks, state[0])
    lane = lax.broadcasted_iota(jnp.int32, (HD, HD), 1)
    groups = tokens // HD
    sums = jnp.zeros((HD, HD), F32)
    att = att_s[...] + dot3((qh[...], ql[...]), pair(bd_h, bd_l, chunks), NN)
    att_s[...] = att
    squares = jnp.sum(att * att, axis=1, keepdims=True)
    cross = jnp.sum(att * sc_s[...], axis=1, keepdims=True)
    for g in range(groups):
        piece = slice(g * HD, (g + 1) * HD)
        sums = jnp.where(lane == g, squares[piece], sums)
        sums = jnp.where(lane == groups + g, cross[piece], sums)
    norm_own[...] = sums.T[: 2 * groups]
    for m in range(1, n_head):
        send(norm_own, norm_in.at[m - 1], 6, head_peer(m))
    both = norm_own[...]
    if n_head > 1:
        wait_in(norm_in, 6)
        for m in range(1, n_head):
            both = both + norm_in[m - 1]
    mean = both / (width * n_head)
    inverse = lax.rsqrt(mean[:groups] + EPS)
    slope = inverse * inverse * inverse * mean[groups:]
    factors = jnp.concatenate(
        [inverse, slope, jnp.zeros((HD - 2 * groups, HD), F32)], axis=0
    ).T
    for g in range(groups):
        piece = slice(g * HD, (g + 1) * HD)
        grad = (
            factors[:, g : g + 1] * sc_s[piece]
            - factors[:, groups + g : groups + g + 1] * att_s[piece]
        )
        gh[piece], gl[piece] = split(grad)

    total = jnp.zeros((heads * HD, HD), F32)
    for c in reversed(range(chunks)):
        here = diagonal(dot3(pair(qh, ql, rows(c)), pair(gh, gl, rows(c)), TN))
        total = total + here
        if c > 0:
            put_block_diagonal(chunks + c, total)
    own[1] = total
    scan_row(1)

    def mix(c):
        for i in range(heads):
            here = (rows(c), cols(i))
            mixing = dot3(pair(gh, gl, *here), pair(vh, vl, *here), NT)
            mixing = split(jnp.where(lower, mixing, 0.0))
            gq_s[here] = dot3(mixing, pair(kh, kl, *here), NN)
            gk_s[here] = dot3(mixing, pair(qh, ql, *here), TN)
            gv_s[here] = dot3(pair(sco_h, sco_l, c, i), pair(gh, gl, *here), TN)
        gq_s[rows(c)] += dot3(pair(gh, gl, rows(c)), pair(bd_h, bd_l, chunks), NT)
        if c > 0:
            gq_s[rows(c)] += dot3(pair(gh, gl, rows(c)), pair(bd_h, bd_l, c - 1), NT)
        if c + 1 < chunks:
            after = pair(bd_h, bd_l, chunks + c + 1)
            gk_s[rows(c)] += dot3(pair(vh, vl, rows(c)), after, NT)
            gv_s[rows(c)] += dot3(pair(kh, kl, rows(c)), after, NN)

    mix(0)
    scan_col(1)
    for c in range(1, chunks):
        mix(c)
    store_q = pltpu.make_async_copy(gq_s, gq_hbm, out_sem.at[0])
    store_q.start()
    scan_back(1)
    scan_end(1)

    put_block_diagonal(2 * chunks, state[1])
    after = pair(bd_h, bd_l, 2 * chunks)
    gk_s[...] += dot3((vh[...], vl[...]), after, NT)
    store_k = pltpu.make_async_copy(gk_s, gk_hbm, out_sem.at[1])
    store_k.start()
    gv_s[...] += dot3((kh[...], kl[...]), after, NN)
    store_v = pltpu.make_async_copy(gv_s, gv_hbm, out_sem.at[2])
    store_v.start()
    for scan in range(2):
        wait_out(row_in.at[scan], 3 * scan)
        if n_y > 1:
            wait_out(col_in.at[scan, pl.ds(0, n_y - 1)], 3 * scan + 1)
        wait_out(row_out.at[scan], 3 * scan + 2)
    if n_head > 1:
        wait_out(norm_in, 6)
    store_q.wait()
    store_k.wait()
    store_v.wait()


def shards(n_seq, n_head, queries, keys, values, cotangent, gain):
    tokens, width = queries.shape
    heads = width // HD
    chunks = tokens // CHUNK
    n_y = n_seq // ROW
    part = heads * HD // ROW
    full = (tokens, width)
    norm_rows = 2 * tokens // HD
    anywhere = pl.BlockSpec(memory_space=pl.ANY)
    out = jax.ShapeDtypeStruct(full, F32)
    return tuple(
        pl.pallas_call(
            functools.partial(body, n_seq, n_head),
            out_shape=(out, out, out),
            in_specs=[anywhere] * 4 + [pl.BlockSpec(memory_space=pltpu.VMEM)],
            out_specs=(anywhere,) * 3,
            scratch_shapes=[pltpu.VMEM(full, F32)] * 8
            + [pltpu.VMEM(full, BF16)] * 8
            + [pltpu.VMEM((chunks, heads, CHUNK, CHUNK), BF16)] * 2
            + [pltpu.VMEM((2 * chunks + 1, width, width), BF16)] * 2
            + [
                pltpu.VMEM((2, heads * HD, HD), F32),
                pltpu.VMEM((2, ROW - 1, part, HD), F32),
                pltpu.VMEM((2, n_y, part, HD), F32),
                pltpu.VMEM((2, ROW - 1, part, HD), F32),
                pltpu.VMEM((2, heads * HD, HD), F32),
                pltpu.VMEM((norm_rows, HD), F32),
                pltpu.VMEM((max(n_head - 1, 1), norm_rows, HD), F32),
                pltpu.SemaphoreType.DMA((4,)),
                pltpu.SemaphoreType.DMA((3,)),
                pltpu.SemaphoreType.DMA((7,)),
                pltpu.SemaphoreType.DMA((7,)),
            ],
            compiler_params=pltpu.CompilerParams(
                collective_id=0, has_side_effects=True
            ),
        )(queries, keys, values, cotangent, gain[None, :])
    )


def solution(mesh):
    in_specs = (P("seq", "head"), P("seq", "head"), P("seq", "head"), P("seq", "head"), P("head"))
    out_specs = (P("seq", "head"), P("seq", "head"), P("seq", "head"))
    return jax.shard_map(
        functools.partial(shards, mesh.shape["seq"], mesh.shape["head"]),
        mesh=mesh,
        in_specs=in_specs,
        out_specs=out_specs,
        check_vma=False,
    )
```

```python
import functools

import jax
import jax.numpy as jnp
from jax import lax
from jax.experimental import pallas as pl
from jax.experimental.pallas import tpu as pltpu
from jax.sharding import PartitionSpec as P

HD = 128
ROW = 8
CHUNK = 256
EPS = 1e-06
MESH = pl.DeviceIdType.MESH
F32 = jnp.float32
BF16 = jnp.bfloat16


def split(x):
    high = x.astype(BF16)
    return high, (x - high.astype(F32)).astype(BF16)


def dot3(left, right, dims):
    def one(a, b):
        return lax.dot_general(a, b, (dims, ((), ())), preferred_element_type=F32)

    (lh, ll), (rh, rl) = left, right
    return one(lh, rh) + (one(lh, rl) + one(ll, rh))


def far_first(count):
    return sorted(range(1, count), key=lambda m: -min(m, count - m))


NN = ((1,), (0,))
NT = ((1,), (1,))
TN = ((0,), (0,))


def body(
    n_seq,
    n_head,
    q_hbm,
    k_hbm,
    v_hbm,
    cot_hbm,
    gain_ref,
    gq_s,
    gk_s,
    gv_s,
    kh,
    kl,
    vh,
    vl,
    after_h,
    after_l,
    q_s,
    k_s,
    v_s,
    sc_s,
    att_s,
    qh,
    ql,
    gh,
    gl,
    sco_h,
    sco_l,
    bd_h,
    bd_l,
    own,
    row_in,
    col_in,
    row_out,
    state,
    norm_own,
    norm_in,
    in_sem,
    send_sem,
    recv_sem,
):
    n_y = n_seq // ROW
    tokens, width = q_s.shape
    heads = width // HD
    chunks = tokens // CHUNK
    part = heads * HD // ROW
    s = lax.axis_index("seq")
    h = lax.axis_index("head")
    j = lax.rem(s, ROW)
    y = lax.div(s, ROW)

    def row_peer(k):
        return (y * ROW + lax.rem(j + k, ROW), h)

    def col_peer(m):
        return (lax.rem(y + m, n_y) * ROW + j, h)

    def head_peer(m):
        return (s, lax.rem(h + m, n_head))

    loads = [
        pltpu.make_async_copy(src, dst, in_sem.at[i])
        for i, (src, dst) in enumerate(
            [(k_hbm, k_s), (v_hbm, v_s), (q_hbm, q_s), (cot_hbm, sc_s)]
        )
    ]
    for load in loads:
        load.start()
    barrier = pltpu.get_barrier_semaphore()
    peers = (
        [row_peer(k) for k in range(1, ROW)]
        + [col_peer(m) for m in range(1, n_y)]
        + [head_peer(m) for m in range(1, n_head)]
    )
    for peer in peers:
        pl.semaphore_signal(barrier, inc=1, device_id=peer, device_id_type=MESH)

    def send(src, dst, stage, peer):
        pltpu.make_async_remote_copy(
            src_ref=src,
            dst_ref=dst,
            send_sem=send_sem.at[stage],
            recv_sem=recv_sem.at[stage],
            device_id=peer,
            device_id_type=MESH,
        ).start()

    def wait_in(ref, stage):
        pltpu.make_async_remote_copy(
            src_ref=ref,
            dst_ref=ref,
            send_sem=send_sem.at[stage],
            recv_sem=recv_sem.at[stage],
            device_id=row_peer(1),
            device_id_type=MESH,
        ).wait_recv()

    def wait_out(ref, stage):
        pltpu.make_async_remote_copy(
            src_ref=ref,
            dst_ref=ref,
            send_sem=send_sem.at[stage],
            recv_sem=recv_sem.at[stage],
            device_id=row_peer(1),
            device_id_type=MESH,
        ).wait_send()

    def weight(cond):
        return jnp.where(cond, 1.0, 0.0).astype(F32)

    def scan_row(scan):
        for k in far_first(ROW):
            there = lax.rem(j + k, ROW)
            send(
                own.at[scan, pl.ds(pl.multiple_of(there * part, part), part)],
                row_in.at[scan, k - 1],
                3 * scan,
                row_peer(k),
            )

    def scan_col(scan):
        wait_in(row_in.at[scan], 3 * scan)
        total = own[scan, pl.ds(pl.multiple_of(j * part, part), part)]
        for k in range(1, ROW):
            total = total + row_in[scan, k - 1]
        col_in[scan, n_y - 1] = total
        for m in far_first(n_y):
            send(
                col_in.at[scan, n_y - 1],
                col_in.at[scan, m - 1],
                3 * scan + 1,
                col_peer(m),
            )

    def scan_back(scan):
        if n_y > 1:
            wait_in(col_in.at[scan, pl.ds(0, n_y - 1)], 3 * scan + 1)
        base = jnp.zeros((part, HD), F32)
        for m in range(1, n_y):
            inside = (y < m) if scan else (y >= m)
            base = base + weight(inside) * col_in[scan, m - 1]
        mine = own[scan, pl.ds(pl.multiple_of(j * part, part), part)]
        for k in far_first(ROW) + [0]:
            there = lax.rem(j + k, ROW)
            value = base
            for r in range(ROW):
                source = lax.rem(j - r + ROW, ROW)
                inside = (source > there) if scan else (source < there)
                piece = mine if r == 0 else row_in[scan, r - 1]
                value = value + weight(inside) * piece
            if k == 0:
                state[scan, pl.ds(pl.multiple_of(j * part, part), part)] = value
            else:
                row_out[scan, k - 1] = value
                send(
                    row_out.at[scan, k - 1],
                    state.at[scan, pl.ds(pl.multiple_of(j * part, part), part)],
                    3 * scan + 2,
                    row_peer(k),
                )

    def scan_end(scan):
        wait_in(state.at[scan, pl.ds(0, (ROW - 1) * part)], 3 * scan + 2)

    def cols(head):
        return slice(head * HD, (head + 1) * HD)

    def rows(chunk):
        return slice(chunk * CHUNK, (chunk + 1) * CHUNK)

    def diagonal(full):
        return jnp.concatenate([full[cols(i), cols(i)] for i in range(heads)], axis=0)

    def put_block_diagonal(slot, stacked):
        high, low = split(stacked)
        for i in range(heads):
            bd_h[slot, cols(i), cols(i)] = high[cols(i)]
            bd_l[slot, cols(i), cols(i)] = low[cols(i)]

    def pair(high, low, *index):
        return high[index], low[index]

    bd_h[...] = jnp.zeros_like(bd_h)
    bd_l[...] = jnp.zeros_like(bd_l)
    lower = lax.broadcasted_iota(jnp.int32, (CHUNK, CHUNK), 0) >= lax.broadcasted_iota(
        jnp.int32, (CHUNK, CHUNK), 1
    )

    loads[0].wait()
    kh[...], kl[...] = split(k_s[...])
    loads[1].wait()
    vh[...], vl[...] = split(v_s[...])
    total = jnp.zeros((heads * HD, HD), F32)
    for c in range(chunks):
        here = diagonal(dot3(pair(kh, kl, rows(c)), pair(vh, vl, rows(c)), TN))
        total = total + here
        if c + 1 < chunks:
            put_block_diagonal(c, total)
    own[0] = total
    pl.semaphore_wait(barrier, len(peers))
    scan_row(0)

    loads[2].wait()
    qh[...], ql[...] = split(q_s[...])
    for c in range(chunks):
        for i in range(heads):
            scores = dot3(
                pair(qh, ql, rows(c), cols(i)), pair(kh, kl, rows(c), cols(i)), NT
            )
            sco_h[c, i], sco_l[c, i] = split(jnp.where(lower, scores, 0.0))
    loads[3].wait()
    sc_s[...] = sc_s[...] * gain_ref[...]
    scan_col(0)
    for c in range(chunks):
        for i in range(heads):
            inner = dot3(pair(sco_h, sco_l, c, i), pair(vh, vl, rows(c), cols(i)), NN)
            att_s[rows(c), cols(i)] = inner
        if c > 0:
            att_s[rows(c)] += dot3(
                pair(qh, ql, rows(c)), pair(bd_h, bd_l, c - 1), NN
            )
    scan_back(0)
    scan_end(0)

    put_block_diagonal(chunks, state[0])
    lane = lax.broadcasted_iota(jnp.int32, (HD, HD), 1)
    groups = tokens // HD
    sums = jnp.zeros((HD, HD), F32)
    att = att_s[...] + dot3((qh[...], ql[...]), pair(bd_h, bd_l, chunks), NN)
    att_s[...] = att
    squares = jnp.sum(att * att, axis=1, keepdims=True)
    cross = jnp.sum(att * sc_s[...], axis=1, keepdims=True)
    for g in range(groups):
        piece = slice(g * HD, (g + 1) * HD)
        sums = jnp.where(lane == g, squares[piece], sums)
        sums = jnp.where(lane == groups + g, cross[piece], sums)
    norm_own[...] = sums.T[: 2 * groups]
    for m in far_first(n_head):
        send(norm_own, norm_in.at[m - 1], 6, head_peer(m))
    both = norm_own[...]
    if n_head > 1:
        wait_in(norm_in, 6)
        for m in range(1, n_head):
            both = both + norm_in[m - 1]
    mean = both / (width * n_head)
    inverse = lax.rsqrt(mean[:groups] + EPS)
    slope = inverse * inverse * inverse * mean[groups:]
    factors = jnp.concatenate(
        [inverse, slope, jnp.zeros((HD - 2 * groups, HD), F32)], axis=0
    ).T
    for g in range(groups):
        piece = slice(g * HD, (g + 1) * HD)
        grad = (
            factors[:, g : g + 1] * sc_s[piece]
            - factors[:, groups + g : groups + g + 1] * att_s[piece]
        )
        gh[piece], gl[piece] = split(grad)

    total = jnp.zeros((heads * HD, HD), F32)
    for c in reversed(range(chunks)):
        here = diagonal(dot3(pair(qh, ql, rows(c)), pair(gh, gl, rows(c)), TN))
        total = total + here
        if c > 0:
            put_block_diagonal(chunks + c, total)
    own[1] = total
    scan_row(1)

    def mix(c):
        for i in range(heads):
            here = (rows(c), cols(i))
            mixing = dot3(pair(gh, gl, *here), pair(vh, vl, *here), NT)
            mixing = split(jnp.where(lower, mixing, 0.0))
            gq_s[here] = dot3(mixing, pair(kh, kl, *here), NN)
            gk_s[here] = dot3(mixing, pair(qh, ql, *here), TN)
            gv_s[here] = dot3(pair(sco_h, sco_l, c, i), pair(gh, gl, *here), TN)
        gq_s[rows(c)] += dot3(pair(gh, gl, rows(c)), pair(bd_h, bd_l, chunks), NT)
        if c > 0:
            gq_s[rows(c)] += dot3(pair(gh, gl, rows(c)), pair(bd_h, bd_l, c - 1), NT)
        if c + 1 < chunks:
            after = pair(bd_h, bd_l, chunks + c + 1)
            gk_s[rows(c)] += dot3(pair(vh, vl, rows(c)), after, NT)
            gv_s[rows(c)] += dot3(pair(kh, kl, rows(c)), after, NN)

    mix(0)
    scan_col(1)
    for c in range(1, chunks):
        mix(c)
    scan_back(1)
    scan_end(1)

    after_h[...] = jnp.zeros_like(after_h)
    after_l[...] = jnp.zeros_like(after_l)
    high, low = split(state[1])
    for i in range(heads):
        after_h[cols(i), cols(i)] = high[cols(i)]
        after_l[cols(i), cols(i)] = low[cols(i)]
    for scan in range(2):
        wait_out(row_in.at[scan], 3 * scan)
        if n_y > 1:
            wait_out(col_in.at[scan, pl.ds(0, n_y - 1)], 3 * scan + 1)
        wait_out(row_out.at[scan], 3 * scan + 2)
    if n_head > 1:
        wait_out(norm_in, 6)


def finish(
    gq_s, gk_s, gv_s, kh, kl, vh, vl, after_h, after_l, gq_hbm, gk_hbm, gv_hbm, k_out, v_out, sem
):
    after = (after_h[...], after_l[...])
    stores = [
        pltpu.make_async_copy(src, dst, sem.at[i])
        for i, (src, dst) in enumerate([(gq_s, gq_hbm), (k_out, gk_hbm), (v_out, gv_hbm)])
    ]
    stores[0].start()
    k_out[...] = gk_s[...] + dot3((vh[...], vl[...]), after, NT)
    stores[1].start()
    v_out[...] = gv_s[...] + dot3((kh[...], kl[...]), after, NN)
    stores[2].start()
    for store in stores:
        store.wait()


def shards(n_seq, n_head, queries, keys, values, cotangent, gain):
    tokens, width = queries.shape
    heads = width // HD
    chunks = tokens // CHUNK
    n_y = n_seq // ROW
    part = heads * HD // ROW
    full = (tokens, width)
    norm_rows = 2 * tokens // HD
    anywhere = pl.BlockSpec(memory_space=pl.ANY)
    vmem = pl.BlockSpec(memory_space=pltpu.VMEM)
    blocks = pl.pallas_call(
        functools.partial(body, n_seq, n_head),
        out_shape=(pltpu.VMEM(full, F32),) * 3
        + (pltpu.VMEM(full, BF16),) * 4
        + (pltpu.VMEM((width, width), BF16),) * 2,
        in_specs=[anywhere] * 4 + [vmem],
        out_specs=(vmem,) * 9,
        scratch_shapes=[pltpu.VMEM(full, F32)] * 5
        + [pltpu.VMEM(full, BF16)] * 4
        + [pltpu.VMEM((chunks, heads, CHUNK, CHUNK), BF16)] * 2
        + [pltpu.VMEM((2 * chunks, width, width), BF16)] * 2
        + [
            pltpu.VMEM((2, heads * HD, HD), F32),
            pltpu.VMEM((2, ROW - 1, part, HD), F32),
            pltpu.VMEM((2, n_y, part, HD), F32),
            pltpu.VMEM((2, ROW - 1, part, HD), F32),
            pltpu.VMEM((2, heads * HD, HD), F32),
            pltpu.VMEM((norm_rows, HD), F32),
            pltpu.VMEM((max(n_head - 1, 1), norm_rows, HD), F32),
            pltpu.SemaphoreType.DMA((4,)),
            pltpu.SemaphoreType.DMA((7,)),
            pltpu.SemaphoreType.DMA((7,)),
        ],
        compiler_params=pltpu.CompilerParams(collective_id=0, has_side_effects=True),
    )(queries, keys, values, cotangent, gain[None, :])
    out = jax.ShapeDtypeStruct(full, F32)
    return tuple(
        pl.pallas_call(
            finish,
            out_shape=(out, out, out),
            in_specs=[vmem] * 9,
            out_specs=(anywhere,) * 3,
            scratch_shapes=[pltpu.VMEM(full, F32)] * 2 + [pltpu.SemaphoreType.DMA((3,))],
        )(*(pltpu.with_memory_space_constraint(b, pltpu.VMEM) for b in blocks))
    )


def solution(mesh):
    in_specs = (P("seq", "head"), P("seq", "head"), P("seq", "head"), P("seq", "head"), P("head"))
    out_specs = (P("seq", "head"), P("seq", "head"), P("seq", "head"))
    return jax.shard_map(
        functools.partial(shards, mesh.shape["seq"], mesh.shape["head"]),
        mesh=mesh,
        in_specs=in_specs,
        out_specs=out_specs,
        check_vma=False,
    )
```

```python
import functools

import jax
import jax.numpy as jnp
from jax import lax
from jax.experimental import pallas as pl
from jax.experimental.pallas import tpu as pltpu
from jax.sharding import PartitionSpec as P

HD = 128
ROW = 8
CHUNK = 256
EPS = 1e-06
MESH = pl.DeviceIdType.MESH
F32 = jnp.float32
BF16 = jnp.bfloat16


def split(x):
    high = x.astype(BF16)
    return high, (x - high.astype(F32)).astype(BF16)


def dot3(left, right, dims):
    def one(a, b):
        return lax.dot_general(a, b, (dims, ((), ())), preferred_element_type=F32)

    (lh, ll), (rh, rl) = left, right
    return one(lh, rh) + (one(lh, rl) + one(ll, rh))


def far_first(count):
    return sorted(range(1, count), key=lambda m: -min(m, count - m))


def relay_steps(count):
    known, steps = 1, []
    while 2 * known + 1 < count:
        step = min(known, count // 2 - known)
        steps.append(step)
        known += step
    return steps


NN = ((1,), (0,))
NT = ((1,), (1,))
TN = ((0,), (0,))


def body(
    n_seq,
    n_head,
    q_hbm,
    k_hbm,
    v_hbm,
    cot_hbm,
    gain_ref,
    gq_s,
    gk_s,
    gv_s,
    kh,
    kl,
    vh,
    vl,
    after_h,
    after_l,
    q_s,
    k_s,
    v_s,
    sc_s,
    att_s,
    qh,
    ql,
    gh,
    gl,
    qt_h,
    qt_l,
    sco_h,
    sco_l,
    bd_h,
    bd_l,
    own,
    row_in,
    col_in,
    row_out,
    state,
    norm_own,
    norm_in,
    in_sem,
    send_sem,
    recv_sem,
    col_sem,
    head_sem,
):
    n_y = n_seq // ROW
    tokens, width = q_s.shape
    heads = width // HD
    chunks = tokens // CHUNK
    part = heads * HD // ROW
    s = lax.axis_index("seq")
    h = lax.axis_index("head")
    j = lax.rem(s, ROW)
    y = lax.div(s, ROW)

    def row_peer(k):
        return (y * ROW + lax.rem(j + k, ROW), h)

    def col_peer(m):
        return (lax.rem(y + m, n_y) * ROW + j, h)

    def head_peer(m):
        return (s, lax.rem(h + m, n_head))

    def near(count, peer):
        return [peer(m) for m in sorted({1, count - 1}) if 0 < m < count]

    barrier = pltpu.get_barrier_semaphore()
    peers = (
        [row_peer(k) for k in far_first(ROW)] + near(n_y, col_peer) + near(n_head, head_peer)
    )
    for peer in peers:
        pl.semaphore_signal(barrier, inc=1, device_id=peer, device_id_type=MESH)
    loads = [
        pltpu.make_async_copy(src, dst, in_sem.at[i])
        for i, (src, dst) in enumerate(
            [(k_hbm, k_s), (v_hbm, v_s), (q_hbm, q_s), (cot_hbm, sc_s)]
        )
    ]
    for load in loads:
        load.start()

    def relay_signal(sem, count, peer, number):
        steps = relay_steps(count)
        if number < len(steps):
            for m in (steps[number], count - steps[number]):
                pl.semaphore_signal(
                    sem.at[number], inc=1, device_id=peer(m), device_id_type=MESH
                )

    def relay_wait(sem, count, number):
        if number < len(relay_steps(count)):
            pl.semaphore_wait(sem.at[number], 2)

    def send(src, dst, stage, peer):
        pltpu.make_async_remote_copy(
            src_ref=src,
            dst_ref=dst,
            send_sem=send_sem.at[stage],
            recv_sem=recv_sem.at[stage],
            device_id=peer,
            device_id_type=MESH,
        ).start()

    def wait_in(ref, stage):
        pltpu.make_async_remote_copy(
            src_ref=ref,
            dst_ref=ref,
            send_sem=send_sem.at[stage],
            recv_sem=recv_sem.at[stage],
            device_id=row_peer(1),
            device_id_type=MESH,
        ).wait_recv()

    def wait_out(ref, stage):
        pltpu.make_async_remote_copy(
            src_ref=ref,
            dst_ref=ref,
            send_sem=send_sem.at[stage],
            recv_sem=recv_sem.at[stage],
            device_id=row_peer(1),
            device_id_type=MESH,
        ).wait_send()

    def weight(cond):
        return jnp.where(cond, 1.0, 0.0).astype(F32)

    def scan_row(scan):
        for k in far_first(ROW):
            there = lax.rem(j + k, ROW)
            send(
                own.at[scan, pl.ds(pl.multiple_of(there * part, part), part)],
                row_in.at[scan, k - 1],
                3 * scan,
                row_peer(k),
            )

    def scan_col(scan):
        wait_in(row_in.at[scan], 3 * scan)
        total = own[scan, pl.ds(pl.multiple_of(j * part, part), part)]
        for k in range(1, ROW):
            total = total + row_in[scan, k - 1]
        col_in[scan, n_y - 1] = total
        if scan == 0:
            relay_wait(col_sem, n_y, 1)
        for m in far_first(n_y):
            send(
                col_in.at[scan, n_y - 1],
                col_in.at[scan, m - 1],
                3 * scan + 1,
                col_peer(m),
            )

    def scan_within(scan):
        for k in far_first(ROW) + [0]:
            there = lax.rem(j + k, ROW)
            value = jnp.zeros((part, HD), F32)
            for r in range(ROW):
                source = lax.rem(j - r + ROW, ROW)
                inside = (source > there) if scan else (source < there)
                piece = (
                    row_in[scan, r - 1]
                    if r
                    else own[scan, pl.ds(pl.multiple_of(j * part, part), part)]
                )
                value = value + weight(inside) * piece
            row_out[scan, k] = value

    def scan_back(scan):
        if n_y > 1:
            wait_in(col_in.at[scan, pl.ds(0, n_y - 1)], 3 * scan + 1)
        base = jnp.zeros((part, HD), F32)
        for m in range(1, n_y):
            inside = (y < m) if scan else (y >= m)
            base = base + weight(inside) * col_in[scan, m - 1]
        here = pl.ds(pl.multiple_of(j * part, part), part)
        for k in far_first(ROW):
            row_out[scan, k] += base
            send(row_out.at[scan, k], state.at[scan, here], 3 * scan + 2, row_peer(k))
        state[scan, here] = row_out[scan, 0] + base

    def scan_end(scan):
        wait_in(state.at[scan, pl.ds(0, (ROW - 1) * part)], 3 * scan + 2)

    def cols(head):
        return slice(head * HD, (head + 1) * HD)

    def rows(chunk):
        return slice(chunk * CHUNK, (chunk + 1) * CHUNK)

    def diagonal(full):
        return jnp.concatenate([full[cols(i), cols(i)] for i in range(heads)], axis=0)

    def put_block_diagonal(slot, stacked):
        high, low = split(stacked)
        for i in range(heads):
            bd_h[slot, cols(i), cols(i)] = high[cols(i)]
            bd_l[slot, cols(i), cols(i)] = low[cols(i)]

    def pair(high, low, *index):
        return high[index], low[index]

    bd_h[...] = jnp.zeros_like(bd_h)
    bd_l[...] = jnp.zeros_like(bd_l)
    lower = lax.broadcasted_iota(jnp.int32, (CHUNK, CHUNK), 0) >= lax.broadcasted_iota(
        jnp.int32, (CHUNK, CHUNK), 1
    )

    loads[0].wait()
    kh[...], kl[...] = split(k_s[...])
    loads[1].wait()
    vh[...], vl[...] = split(v_s[...])
    total = jnp.zeros((heads * HD, HD), F32)
    for c in range(chunks):
        here = diagonal(dot3(pair(kh, kl, rows(c)), pair(vh, vl, rows(c)), TN))
        total = total + here
        if c + 1 < chunks:
            put_block_diagonal(c, total)
    own[0] = total
    pl.semaphore_wait(barrier, len(peers))
    relay_signal(col_sem, n_y, col_peer, 0)
    relay_signal(head_sem, n_head, head_peer, 0)
    scan_row(0)

    loads[2].wait()
    qh[...], ql[...] = split(q_s[...])
    for c in range(chunks):
        for i in range(heads):
            scores = dot3(
                pair(qh, ql, rows(c), cols(i)), pair(kh, kl, rows(c), cols(i)), NT
            )
            sco_h[c, i], sco_l[c, i] = split(jnp.where(lower, scores, 0.0))
        if c == 0:
            relay_wait(col_sem, n_y, 0)
            relay_signal(col_sem, n_y, col_peer, 1)
            relay_wait(head_sem, n_head, 0)
            relay_signal(head_sem, n_head, head_peer, 1)
    loads[3].wait()
    sc_s[...] = sc_s[...] * gain_ref[...]
    scan_col(0)
    relay_wait(head_sem, n_head, 1)
    relay_signal(head_sem, n_head, head_peer, 2)
    scan_within(0)
    qt_h[...], qt_l[...] = split(q_s[...].T)
    for c in range(chunks):
        for i in range(heads):
            inner = dot3(pair(sco_h, sco_l, c, i), pair(vh, vl, rows(c), cols(i)), NN)
            att_s[rows(c), cols(i)] = inner
        if c > 0:
            att_s[rows(c)] += dot3(
                pair(qh, ql, rows(c)), pair(bd_h, bd_l, c - 1), NN
            )
    scan_back(0)
    scan_end(0)

    put_block_diagonal(chunks, state[0])
    lane = lax.broadcasted_iota(jnp.int32, (HD, HD), 1)
    groups = tokens // HD
    sums = jnp.zeros((HD, HD), F32)
    att = att_s[...] + dot3((qh[...], ql[...]), pair(bd_h, bd_l, chunks), NN)
    att_s[...] = att
    squares = jnp.sum(att * att, axis=1, keepdims=True)
    cross = jnp.sum(att * sc_s[...], axis=1, keepdims=True)
    for g in range(groups):
        piece = slice(g * HD, (g + 1) * HD)
        sums = jnp.where(lane == g, squares[piece], sums)
        sums = jnp.where(lane == groups + g, cross[piece], sums)
    norm_own[...] = sums.T[: 2 * groups]
    relay_wait(head_sem, n_head, 2)
    for m in far_first(n_head):
        send(norm_own, norm_in.at[m - 1], 6, head_peer(m))
    both = norm_own[...]
    if n_head > 1:
        wait_in(norm_in, 6)
        for m in range(1, n_head):
            both = both + norm_in[m - 1]
    mean = both / (width * n_head)
    inverse = lax.rsqrt(mean[:groups] + EPS)
    slope = inverse * inverse * inverse * mean[groups:]
    factors = jnp.concatenate(
        [inverse, slope, jnp.zeros((HD - 2 * groups, HD), F32)], axis=0
    ).T
    for g in range(groups):
        piece = slice(g * HD, (g + 1) * HD)
        grad = (
            factors[:, g : g + 1] * sc_s[piece]
            - factors[:, groups + g : groups + g + 1] * att_s[piece]
        )
        gh[piece], gl[piece] = split(grad)

    total = jnp.zeros((heads * HD, HD), F32)
    for c in reversed(range(chunks)):
        here = diagonal(
            dot3((qt_h[:, rows(c)], qt_l[:, rows(c)]), pair(gh, gl, rows(c)), NN)
        )
        total = total + here
        if c > 0:
            put_block_diagonal(chunks + c, total)
    own[1] = total
    scan_row(1)

    def mix(c):
        for i in range(heads):
            here = (rows(c), cols(i))
            mixing = dot3(pair(gh, gl, *here), pair(vh, vl, *here), NT)
            mixing = split(jnp.where(lower, mixing, 0.0))
            gq_s[here] = dot3(mixing, pair(kh, kl, *here), NN)
            gk_s[here] = dot3(mixing, pair(qh, ql, *here), TN)
            gv_s[here] = dot3(pair(sco_h, sco_l, c, i), pair(gh, gl, *here), TN)
        gq_s[rows(c)] += dot3(pair(gh, gl, rows(c)), pair(bd_h, bd_l, chunks), NT)
        if c > 0:
            gq_s[rows(c)] += dot3(pair(gh, gl, rows(c)), pair(bd_h, bd_l, c - 1), NT)
        if c + 1 < chunks:
            after = pair(bd_h, bd_l, chunks + c + 1)
            gk_s[rows(c)] += dot3(pair(vh, vl, rows(c)), after, NT)
            gv_s[rows(c)] += dot3(pair(kh, kl, rows(c)), after, NN)

    mix(0)
    scan_col(1)
    scan_within(1)
    for c in range(1, chunks):
        mix(c)
    scan_back(1)
    scan_end(1)

    after_h[...] = jnp.zeros_like(after_h)
    after_l[...] = jnp.zeros_like(after_l)
    high, low = split(state[1])
    for i in range(heads):
        after_h[cols(i), cols(i)] = high[cols(i)]
        after_l[cols(i), cols(i)] = low[cols(i)]
    for scan in range(2):
        wait_out(row_in.at[scan], 3 * scan)
        if n_y > 1:
            wait_out(col_in.at[scan, pl.ds(0, n_y - 1)], 3 * scan + 1)
        wait_out(row_out.at[scan, pl.ds(1, ROW - 1)], 3 * scan + 2)
    if n_head > 1:
        wait_out(norm_in, 6)


def finish(
    gq_s, gk_s, gv_s, kh, kl, vh, vl, after_h, after_l, gq_hbm, gk_hbm, gv_hbm, k_out, v_out, sem
):
    after = (after_h[...], after_l[...])
    stores = [
        pltpu.make_async_copy(src, dst, sem.at[i])
        for i, (src, dst) in enumerate([(gq_s, gq_hbm), (k_out, gk_hbm), (v_out, gv_hbm)])
    ]
    stores[0].start()
    k_out[...] = gk_s[...] + dot3((vh[...], vl[...]), after, NT)
    stores[1].start()
    v_out[...] = gv_s[...] + dot3((kh[...], kl[...]), after, NN)
    stores[2].start()
    for store in stores:
        store.wait()


def shards(n_seq, n_head, queries, keys, values, cotangent, gain):
    tokens, width = queries.shape
    heads = width // HD
    chunks = tokens // CHUNK
    n_y = n_seq // ROW
    part = heads * HD // ROW
    full = (tokens, width)
    norm_rows = 2 * tokens // HD
    anywhere = pl.BlockSpec(memory_space=pl.ANY)
    vmem = pl.BlockSpec(memory_space=pltpu.VMEM)
    blocks = pl.pallas_call(
        functools.partial(body, n_seq, n_head),
        out_shape=(pltpu.VMEM(full, F32),) * 3
        + (pltpu.VMEM(full, BF16),) * 4
        + (pltpu.VMEM((width, width), BF16),) * 2,
        in_specs=[anywhere] * 4 + [vmem],
        out_specs=(vmem,) * 9,
        scratch_shapes=[pltpu.VMEM(full, F32)] * 5
        + [pltpu.VMEM(full, BF16)] * 4
        + [pltpu.VMEM((width, tokens), BF16)] * 2
        + [pltpu.VMEM((chunks, heads, CHUNK, CHUNK), BF16)] * 2
        + [pltpu.VMEM((2 * chunks, width, width), BF16)] * 2
        + [
            pltpu.VMEM((2, heads * HD, HD), F32),
            pltpu.VMEM((2, ROW - 1, part, HD), F32),
            pltpu.VMEM((2, n_y, part, HD), F32),
            pltpu.VMEM((2, ROW, part, HD), F32),
            pltpu.VMEM((2, heads * HD, HD), F32),
            pltpu.VMEM((norm_rows, HD), F32),
            pltpu.VMEM((max(n_head - 1, 1), norm_rows, HD), F32),
            pltpu.SemaphoreType.DMA((4,)),
            pltpu.SemaphoreType.DMA((7,)),
            pltpu.SemaphoreType.DMA((7,)),
            pltpu.SemaphoreType.REGULAR((3,)),
            pltpu.SemaphoreType.REGULAR((3,)),
        ],
        compiler_params=pltpu.CompilerParams(collective_id=0, has_side_effects=True),
    )(queries, keys, values, cotangent, gain[None, :])
    out = jax.ShapeDtypeStruct(full, F32)
    return tuple(
        pl.pallas_call(
            finish,
            out_shape=(out, out, out),
            in_specs=[vmem] * 9,
            out_specs=(anywhere,) * 3,
            scratch_shapes=[pltpu.VMEM(full, F32)] * 2 + [pltpu.SemaphoreType.DMA((3,))],
        )(*(pltpu.with_memory_space_constraint(b, pltpu.VMEM) for b in blocks))
    )


def solution(mesh):
    in_specs = (P("seq", "head"), P("seq", "head"), P("seq", "head"), P("seq", "head"), P("head"))
    out_specs = (P("seq", "head"), P("seq", "head"), P("seq", "head"))
    return jax.shard_map(
        functools.partial(shards, mesh.shape["seq"], mesh.shape["head"]),
        mesh=mesh,
        in_specs=in_specs,
        out_specs=out_specs,
        check_vma=False,
    )
```

```python
import functools

import jax
import jax.numpy as jnp
from jax import lax
from jax.experimental import pallas as pl
from jax.experimental.pallas import tpu as pltpu
from jax.sharding import PartitionSpec as P

HD = 128
ROW = 8
CHUNK = 256
EPS = 1e-06
MESH = pl.DeviceIdType.MESH
F32 = jnp.float32
BF16 = jnp.bfloat16


def split(x):
    high = x.astype(BF16)
    return high, (x - high.astype(F32)).astype(BF16)


def dot3(left, right, dims):
    def one(a, b):
        return lax.dot_general(a, b, (dims, ((), ())), preferred_element_type=F32)

    (lh, ll), (rh, rl) = left, right
    return one(lh, rh) + (one(lh, rl) + one(ll, rh))


def far_first(count):
    return sorted(range(1, count), key=lambda m: -min(m, count - m))


def row_order(count):
    return sorted(range(1, count), key=lambda k: -(min(k, count - k) + 1.5 * (k % 2)))


def relay_steps(count):
    known, steps = 1, []
    while 2 * known + 1 < count:
        step = min(known, count // 2 - known)
        steps.append(step)
        known += step
    return steps


NN = ((1,), (0,))
NT = ((1,), (1,))
TN = ((0,), (0,))


def body(
    n_seq,
    n_head,
    q_hbm,
    k_hbm,
    v_hbm,
    cot_hbm,
    gain_hbm,
    gq_s,
    gk_s,
    gv_s,
    kh,
    kl,
    vh,
    vl,
    after_h,
    after_l,
    q_s,
    k_s,
    v_s,
    sc_s,
    gain_s,
    att_s,
    qh,
    ql,
    gh,
    gl,
    qt_h,
    qt_l,
    sco_h,
    sco_l,
    bd_h,
    bd_l,
    own,
    row_in,
    col_in,
    row_out,
    state,
    norm_own,
    norm_in,
    in_sem,
    send_sem,
    recv_sem,
    col_send,
    col_recv,
    col_sem,
    head_sem,
):
    n_y = n_seq // ROW
    tokens, width = q_s.shape
    heads = width // HD
    chunks = tokens // CHUNK
    part = heads * HD // ROW
    s = lax.axis_index("seq")
    h = lax.axis_index("head")
    j = lax.rem(s, ROW)
    y = lax.div(s, ROW)

    def row_peer(k):
        return (y * ROW + lax.rem(j + k, ROW), h)

    def col_peer(m):
        return (lax.rem(y + m, n_y) * ROW + j, h)

    def head_peer(m):
        return (s, lax.rem(h + m, n_head))

    def near(count, peer):
        return [peer(m) for m in sorted({1, count - 1}) if 0 < m < count]

    barrier = pltpu.get_barrier_semaphore()
    peers = (
        [row_peer(k) for k in row_order(ROW)] + near(n_y, col_peer) + near(n_head, head_peer)
    )
    for peer in peers:
        pl.semaphore_signal(barrier, inc=1, device_id=peer, device_id_type=MESH)
    loads = [
        pltpu.make_async_copy(src, dst, in_sem.at[i])
        for i, (src, dst) in enumerate(
            [(k_hbm, k_s), (v_hbm, v_s), (q_hbm, q_s), (cot_hbm, sc_s), (gain_hbm, gain_s)]
        )
    ]
    for load in loads:
        load.start()

    def relay_signal(sem, count, peer, number):
        steps = relay_steps(count)
        if number < len(steps):
            for m in (steps[number], count - steps[number]):
                pl.semaphore_signal(
                    sem.at[number], inc=1, device_id=peer(m), device_id_type=MESH
                )

    def relay_wait(sem, count, number):
        if number < len(relay_steps(count)):
            pl.semaphore_wait(sem.at[number], 2)

    def remote(src, dst, sems, peer):
        return pltpu.make_async_remote_copy(
            src_ref=src,
            dst_ref=dst,
            send_sem=sems[0],
            recv_sem=sems[1],
            device_id=peer,
            device_id_type=MESH,
        )

    def sems(stage):
        return send_sem.at[stage], recv_sem.at[stage]

    def send(src, dst, stage, peer):
        remote(src, dst, sems(stage), peer).start()

    def wait_in(ref, stage):
        remote(ref, ref, sems(stage), row_peer(1)).wait_recv()

    def wait_out(ref, stage):
        remote(ref, ref, sems(stage), row_peer(1)).wait_send()

    def col_copy(scan, m):
        return remote(
            col_in.at[scan, n_y - 1],
            col_in.at[scan, m - 1],
            (col_send.at[scan, m - 1], col_recv.at[scan, m - 1]),
            col_peer(m),
        )

    def goes(scan, m):
        return (y + m >= n_y) if scan else (y + m < n_y)

    def comes(scan, m):
        return (y < m) if scan else (y >= m)

    def weight(cond):
        return jnp.where(cond, 1.0, 0.0).astype(F32)

    def scan_row(scan):
        for k in row_order(ROW):
            there = lax.rem(j + k, ROW)
            send(
                own.at[scan, pl.ds(pl.multiple_of(there * part, part), part)],
                row_in.at[scan, k - 1],
                2 * scan,
                row_peer(k),
            )

    def scan_col(scan):
        wait_in(row_in.at[scan], 2 * scan)
        total = own[scan, pl.ds(pl.multiple_of(j * part, part), part)]
        for k in range(1, ROW):
            total = total + row_in[scan, k - 1]
        col_in[scan, n_y - 1] = total
        if scan == 0:
            relay_wait(col_sem, n_y, 1)
        for m in far_first(n_y):

            @pl.when(goes(scan, m))
            def _():
                col_copy(scan, m).start()

    def scan_within(scan):
        for k in row_order(ROW) + [0]:
            there = lax.rem(j + k, ROW)
            value = jnp.zeros((part, HD), F32)
            for r in range(ROW):
                source = lax.rem(j - r + ROW, ROW)
                inside = (source > there) if scan else (source < there)
                piece = (
                    row_in[scan, r - 1]
                    if r
                    else own[scan, pl.ds(pl.multiple_of(j * part, part), part)]
                )
                value = value + weight(inside) * piece
            row_out[scan, k] = value

    def scan_back(scan):
        for m in range(1, n_y):

            @pl.when(comes(scan, m))
            def _():
                col_copy(scan, m).wait_recv()

        base = jnp.zeros((part, HD), F32)
        for m in range(1, n_y):
            base = base + jnp.where(comes(scan, m), col_in[scan, m - 1], 0.0)
        here = pl.ds(pl.multiple_of(j * part, part), part)
        for k in row_order(ROW):
            row_out[scan, k] += base
            send(row_out.at[scan, k], state.at[scan, here], 2 * scan + 1, row_peer(k))
        state[scan, here] = row_out[scan, 0] + base

    def scan_end(scan):
        wait_in(state.at[scan, pl.ds(0, (ROW - 1) * part)], 2 * scan + 1)

    def cols(head):
        return slice(head * HD, (head + 1) * HD)

    def rows(chunk):
        return slice(chunk * CHUNK, (chunk + 1) * CHUNK)

    def diagonal(full):
        return jnp.concatenate([full[cols(i), cols(i)] for i in range(heads)], axis=0)

    def put_block_diagonal(slot, stacked):
        high, low = split(stacked)
        for i in range(heads):
            bd_h[slot, cols(i), cols(i)] = high[cols(i)]
            bd_l[slot, cols(i), cols(i)] = low[cols(i)]

    def pair(high, low, *index):
        return high[index], low[index]

    bd_h[...] = jnp.zeros_like(bd_h)
    bd_l[...] = jnp.zeros_like(bd_l)
    lower = lax.broadcasted_iota(jnp.int32, (CHUNK, CHUNK), 0) >= lax.broadcasted_iota(
        jnp.int32, (CHUNK, CHUNK), 1
    )

    loads[0].wait()
    kh[...], kl[...] = split(k_s[...])
    loads[1].wait()
    vh[...], vl[...] = split(v_s[...])
    total = jnp.zeros((heads * HD, HD), F32)
    for c in range(chunks):
        here = diagonal(dot3(pair(kh, kl, rows(c)), pair(vh, vl, rows(c)), TN))
        total = total + here
        if c + 1 < chunks:
            put_block_diagonal(c, total)
    own[0] = total
    pl.semaphore_wait(barrier, len(peers))
    relay_signal(col_sem, n_y, col_peer, 0)
    relay_signal(head_sem, n_head, head_peer, 0)
    scan_row(0)

    loads[2].wait()
    qh[...], ql[...] = split(q_s[...])
    for c in range(chunks):
        for i in range(heads):
            scores = dot3(
                pair(qh, ql, rows(c), cols(i)), pair(kh, kl, rows(c), cols(i)), NT
            )
            sco_h[c, i], sco_l[c, i] = split(jnp.where(lower, scores, 0.0))
        if c == 0:
            relay_wait(col_sem, n_y, 0)
            relay_signal(col_sem, n_y, col_peer, 1)
            relay_wait(head_sem, n_head, 0)
            relay_signal(head_sem, n_head, head_peer, 1)
    loads[3].wait()
    loads[4].wait()
    sc_s[...] = sc_s[...] * gain_s[...]
    scan_col(0)
    relay_wait(head_sem, n_head, 1)
    relay_signal(head_sem, n_head, head_peer, 2)
    scan_within(0)
    qt_h[...], qt_l[...] = split(q_s[...].T)
    for c in range(chunks):
        for i in range(heads):
            inner = dot3(pair(sco_h, sco_l, c, i), pair(vh, vl, rows(c), cols(i)), NN)
            att_s[rows(c), cols(i)] = inner
        if c > 0:
            att_s[rows(c)] += dot3(
                pair(qh, ql, rows(c)), pair(bd_h, bd_l, c - 1), NN
            )
    scan_back(0)
    scan_end(0)

    put_block_diagonal(chunks, state[0])
    lane = lax.broadcasted_iota(jnp.int32, (HD, HD), 1)
    groups = tokens // HD
    sums = jnp.zeros((HD, HD), F32)
    att = att_s[...] + dot3((qh[...], ql[...]), pair(bd_h, bd_l, chunks), NN)
    att_s[...] = att
    squares = jnp.sum(att * att, axis=1, keepdims=True)
    cross = jnp.sum(att * sc_s[...], axis=1, keepdims=True)
    for g in range(groups):
        piece = slice(g * HD, (g + 1) * HD)
        sums = jnp.where(lane == g, squares[piece], sums)
        sums = jnp.where(lane == groups + g, cross[piece], sums)
    norm_own[...] = sums.T[: 2 * groups]
    relay_wait(head_sem, n_head, 2)
    for m in far_first(n_head):
        send(norm_own, norm_in.at[m - 1], 4, head_peer(m))
    both = norm_own[...]
    if n_head > 1:
        wait_in(norm_in, 4)
        for m in range(1, n_head):
            both = both + norm_in[m - 1]
    mean = both / (width * n_head)
    inverse = lax.rsqrt(mean[:groups] + EPS)
    slope = inverse * inverse * inverse * mean[groups:]
    factors = jnp.concatenate(
        [inverse, slope, jnp.zeros((HD - 2 * groups, HD), F32)], axis=0
    ).T
    for g in range(groups):
        piece = slice(g * HD, (g + 1) * HD)
        grad = (
            factors[:, g : g + 1] * sc_s[piece]
            - factors[:, groups + g : groups + g + 1] * att_s[piece]
        )
        gh[piece], gl[piece] = split(grad)

    total = jnp.zeros((heads * HD, HD), F32)
    for c in reversed(range(chunks)):
        here = diagonal(
            dot3((qt_h[:, rows(c)], qt_l[:, rows(c)]), pair(gh, gl, rows(c)), NN)
        )
        total = total + here
        if c > 0:
            put_block_diagonal(chunks + c, total)
    own[1] = total
    scan_row(1)

    def mix(c):
        for i in range(heads):
            here = (rows(c), cols(i))
            mixing = dot3(pair(gh, gl, *here), pair(vh, vl, *here), NT)
            mixing = split(jnp.where(lower, mixing, 0.0))
            gq_s[here] = dot3(mixing, pair(kh, kl, *here), NN)
            gk_s[here] = dot3(mixing, pair(qh, ql, *here), TN)
            gv_s[here] = dot3(pair(sco_h, sco_l, c, i), pair(gh, gl, *here), TN)
        gq_s[rows(c)] += dot3(pair(gh, gl, rows(c)), pair(bd_h, bd_l, chunks), NT)
        if c > 0:
            gq_s[rows(c)] += dot3(pair(gh, gl, rows(c)), pair(bd_h, bd_l, c - 1), NT)
        if c + 1 < chunks:
            after = pair(bd_h, bd_l, chunks + c + 1)
            gk_s[rows(c)] += dot3(pair(vh, vl, rows(c)), after, NT)
            gv_s[rows(c)] += dot3(pair(kh, kl, rows(c)), after, NN)

    mix(0)
    scan_col(1)
    scan_within(1)
    for c in range(1, chunks):
        mix(c)
    scan_back(1)
    scan_end(1)

    after_h[...] = jnp.zeros_like(after_h)
    after_l[...] = jnp.zeros_like(after_l)
    high, low = split(state[1])
    for i in range(heads):
        after_h[cols(i), cols(i)] = high[cols(i)]
        after_l[cols(i), cols(i)] = low[cols(i)]
    for scan in range(2):
        wait_out(row_in.at[scan], 2 * scan)
        for m in range(1, n_y):

            @pl.when(goes(scan, m))
            def _():
                col_copy(scan, m).wait_send()

        wait_out(row_out.at[scan, pl.ds(1, ROW - 1)], 2 * scan + 1)
    if n_head > 1:
        wait_out(norm_in, 4)


def finish(
    gq_s, gk_s, gv_s, kh, kl, vh, vl, after_h, after_l, gq_hbm, gk_hbm, gv_hbm, k_out, v_out, sem
):
    after = (after_h[...], after_l[...])
    stores = [pltpu.make_async_copy(gq_s, gq_hbm, sem.at[0])]
    stores[0].start()

    def store(src, dst, piece):
        stores.append(pltpu.make_async_copy(src.at[piece], dst.at[piece], sem.at[len(stores)]))
        stores[-1].start()

    for c in range(gq_s.shape[0] // CHUNK):
        piece = pl.ds(c * CHUNK, CHUNK)
        k_out[piece] = gk_s[piece] + dot3((vh[piece], vl[piece]), after, NT)
        store(k_out, gk_hbm, piece)
        v_out[piece] = gv_s[piece] + dot3((kh[piece], kl[piece]), after, NN)
        store(v_out, gv_hbm, piece)
    for copy in stores:
        copy.wait()


def shards(n_seq, n_head, queries, keys, values, cotangent, gain):
    tokens, width = queries.shape
    heads = width // HD
    chunks = tokens // CHUNK
    n_y = n_seq // ROW
    part = heads * HD // ROW
    full = (tokens, width)
    norm_rows = 2 * tokens // HD
    anywhere = pl.BlockSpec(memory_space=pl.ANY)
    vmem = pl.BlockSpec(memory_space=pltpu.VMEM)
    blocks = pl.pallas_call(
        functools.partial(body, n_seq, n_head),
        out_shape=(pltpu.VMEM(full, F32),) * 3
        + (pltpu.VMEM(full, BF16),) * 4
        + (pltpu.VMEM((width, width), BF16),) * 2,
        in_specs=[anywhere] * 5,
        out_specs=(vmem,) * 9,
        scratch_shapes=[pltpu.VMEM(full, F32)] * 4
        + [pltpu.VMEM((1, width), F32), pltpu.VMEM(full, F32)]
        + [pltpu.VMEM(full, BF16)] * 4
        + [pltpu.VMEM((width, tokens), BF16)] * 2
        + [pltpu.VMEM((chunks, heads, CHUNK, CHUNK), BF16)] * 2
        + [pltpu.VMEM((2 * chunks, width, width), BF16)] * 2
        + [
            pltpu.VMEM((2, heads * HD, HD), F32),
            pltpu.VMEM((2, ROW - 1, part, HD), F32),
            pltpu.VMEM((2, n_y, part, HD), F32),
            pltpu.VMEM((2, ROW, part, HD), F32),
            pltpu.VMEM((2, heads * HD, HD), F32),
            pltpu.VMEM((norm_rows, HD), F32),
            pltpu.VMEM((max(n_head - 1, 1), norm_rows, HD), F32),
            pltpu.SemaphoreType.DMA((5,)),
            pltpu.SemaphoreType.DMA((5,)),
            pltpu.SemaphoreType.DMA((5,)),
            pltpu.SemaphoreType.DMA((2, max(n_y - 1, 1))),
            pltpu.SemaphoreType.DMA((2, max(n_y - 1, 1))),
            pltpu.SemaphoreType.REGULAR((3,)),
            pltpu.SemaphoreType.REGULAR((3,)),
        ],
        compiler_params=pltpu.CompilerParams(collective_id=0, has_side_effects=True),
    )(queries, keys, values, cotangent, gain[None, :])
    out = jax.ShapeDtypeStruct(full, F32)
    return tuple(
        pl.pallas_call(
            finish,
            out_shape=(out, out, out),
            in_specs=[vmem] * 9,
            out_specs=(anywhere,) * 3,
            scratch_shapes=[pltpu.VMEM(full, F32)] * 2 + [pltpu.SemaphoreType.DMA((1 + 2 * chunks,))],
        )(*(pltpu.with_memory_space_constraint(b, pltpu.VMEM) for b in blocks))
    )


def solution(mesh):
    in_specs = (P("seq", "head"), P("seq", "head"), P("seq", "head"), P("seq", "head"), P("head"))
    out_specs = (P("seq", "head"), P("seq", "head"), P("seq", "head"))
    return jax.shard_map(
        functools.partial(shards, mesh.shape["seq"], mesh.shape["head"]),
        mesh=mesh,
        in_specs=in_specs,
        out_specs=out_specs,
        check_vma=False,
    )
```

```python
import functools

import jax
import jax.numpy as jnp
from jax import lax
from jax.experimental import pallas as pl
from jax.experimental.pallas import tpu as pltpu
from jax.sharding import PartitionSpec as P

HD = 128
ROW = 8
CHUNK = 256
EPS = 1e-06
MESH = pl.DeviceIdType.MESH
F32 = jnp.float32
BF16 = jnp.bfloat16


def split(x):
    high = x.astype(BF16)
    return high, (x - high.astype(F32)).astype(BF16)


def dot3(left, right, dims):
    def one(a, b):
        return lax.dot_general(a, b, (dims, ((), ())), preferred_element_type=F32)

    (lh, ll), (rh, rl) = left, right
    return one(lh, rh) + (one(lh, rl) + one(ll, rh))


def far_first(count):
    return sorted(range(1, count), key=lambda m: -min(m, count - m))


def row_order(count):
    return sorted(range(1, count), key=lambda k: -(min(k, count - k) + 1.5 * (k % 2)))


def relay_steps(count):
    known, steps = 1, []
    while 2 * known + 1 < count:
        step = min(known, count // 2 - known)
        steps.append(step)
        known += step
    return steps


NN = ((1,), (0,))
NT = ((1,), (1,))
TN = ((0,), (0,))


def body(
    n_seq,
    n_head,
    q_hbm,
    k_hbm,
    v_hbm,
    cot_hbm,
    gain_hbm,
    gq_s,
    gk_s,
    gv_s,
    kh,
    kl,
    vh,
    vl,
    after_h,
    after_l,
    q_s,
    k_s,
    v_s,
    sc_s,
    gain_s,
    att_s,
    qh,
    ql,
    gh,
    gl,
    qt_h,
    qt_l,
    sco_h,
    sco_l,
    bd_h,
    bd_l,
    own,
    row_in,
    col_in,
    row_out,
    state,
    norm_own,
    norm_in,
    in_sem,
    send_sem,
    recv_sem,
    col_send,
    col_recv,
    col_sem,
    head_sem,
):
    n_y = n_seq // ROW
    tokens, width = q_s.shape
    heads = width // HD
    chunks = tokens // CHUNK
    part = heads * HD // ROW
    s = lax.axis_index("seq")
    h = lax.axis_index("head")
    j = lax.rem(s, ROW)
    y = lax.div(s, ROW)

    def row_peer(k):
        return (y * ROW + lax.rem(j + k, ROW), h)

    def col_peer(m):
        return (lax.rem(y + m, n_y) * ROW + j, h)

    def head_peer(m):
        return (s, lax.rem(h + m, n_head))

    def near(count, peer):
        return [peer(m) for m in sorted({1, count - 1}) if 0 < m < count]

    barrier = pltpu.get_barrier_semaphore()
    peers = (
        [row_peer(k) for k in row_order(ROW)] + near(n_y, col_peer) + near(n_head, head_peer)
    )
    for peer in peers:
        pl.semaphore_signal(barrier, inc=1, device_id=peer, device_id_type=MESH)
    loads = [
        pltpu.make_async_copy(src, dst, in_sem.at[i])
        for i, (src, dst) in enumerate(
            [(k_hbm, k_s), (v_hbm, v_s), (q_hbm, q_s), (cot_hbm, sc_s), (gain_hbm, gain_s)]
        )
    ]
    for load in loads:
        load.start()

    def relay_signal(sem, count, peer, number):
        steps = relay_steps(count)
        if number < len(steps):
            for m in (steps[number], count - steps[number]):
                pl.semaphore_signal(
                    sem.at[number], inc=1, device_id=peer(m), device_id_type=MESH
                )

    def relay_wait(sem, count, number):
        if number < len(relay_steps(count)):
            pl.semaphore_wait(sem.at[number], 2)

    def remote(src, dst, sems, peer):
        return pltpu.make_async_remote_copy(
            src_ref=src,
            dst_ref=dst,
            send_sem=sems[0],
            recv_sem=sems[1],
            device_id=peer,
            device_id_type=MESH,
        )

    def sems(stage):
        return send_sem.at[stage], recv_sem.at[stage]

    def send(src, dst, stage, peer):
        remote(src, dst, sems(stage), peer).start()

    def wait_in(ref, stage):
        remote(ref, ref, sems(stage), row_peer(1)).wait_recv()

    def wait_out(ref, stage):
        remote(ref, ref, sems(stage), row_peer(1)).wait_send()

    def col_copy(scan, m):
        return remote(
            col_in.at[scan, n_y - 1],
            col_in.at[scan, m - 1],
            (col_send.at[scan, m - 1], col_recv.at[scan, m - 1]),
            col_peer(m),
        )

    def goes(scan, m):
        return (y + m >= n_y) if scan else (y + m < n_y)

    def comes(scan, m):
        return (y < m) if scan else (y >= m)

    def weight(cond):
        return jnp.where(cond, 1.0, 0.0).astype(F32)

    def scan_row(scan):
        for k in row_order(ROW):
            there = lax.rem(j + k, ROW)
            send(
                own.at[scan, pl.ds(pl.multiple_of(there * part, part), part)],
                row_in.at[scan, k - 1],
                2 * scan,
                row_peer(k),
            )

    def scan_col(scan):
        wait_in(row_in.at[scan], 2 * scan)
        total = own[scan, pl.ds(pl.multiple_of(j * part, part), part)]
        for k in range(1, ROW):
            total = total + row_in[scan, k - 1]
        col_in[scan, n_y - 1] = total
        if scan == 0:
            relay_wait(col_sem, n_y, 1)
        for m in far_first(n_y):

            @pl.when(goes(scan, m))
            def _():
                col_copy(scan, m).start()

    def scan_within(scan):
        for k in row_order(ROW) + [0]:
            there = lax.rem(j + k, ROW)
            value = jnp.zeros((part, HD), F32)
            for r in range(ROW):
                source = lax.rem(j - r + ROW, ROW)
                inside = (source > there) if scan else (source < there)
                piece = (
                    row_in[scan, r - 1]
                    if r
                    else own[scan, pl.ds(pl.multiple_of(j * part, part), part)]
                )
                value = value + weight(inside) * piece
            row_out[scan, k] = value

    def scan_back(scan):
        base = jnp.zeros((part, HD), F32)
        for m in reversed(far_first(n_y)):

            @pl.when(comes(scan, m))
            def _():
                col_copy(scan, m).wait_recv()

            base = base + jnp.where(comes(scan, m), col_in[scan, m - 1], 0.0)
        here = pl.ds(pl.multiple_of(j * part, part), part)
        for k in row_order(ROW):
            row_out[scan, k] += base
            send(row_out.at[scan, k], state.at[scan, here], 2 * scan + 1, row_peer(k))
        state[scan, here] = row_out[scan, 0] + base

    def sent(scan):
        wait_out(row_in.at[scan], 2 * scan)
        for m in range(1, n_y):

            @pl.when(goes(scan, m))
            def _():
                col_copy(scan, m).wait_send()

    def scan_end(scan):
        wait_in(state.at[scan, pl.ds(0, (ROW - 1) * part)], 2 * scan + 1)

    def cols(head):
        return slice(head * HD, (head + 1) * HD)

    def rows(chunk):
        return slice(chunk * CHUNK, (chunk + 1) * CHUNK)

    def diagonal(full):
        return jnp.concatenate([full[cols(i), cols(i)] for i in range(heads)], axis=0)

    def put_block_diagonal(slot, stacked):
        high, low = split(stacked)
        for i in range(heads):
            bd_h[slot, cols(i), cols(i)] = high[cols(i)]
            bd_l[slot, cols(i), cols(i)] = low[cols(i)]

    def pair(high, low, *index):
        return high[index], low[index]

    bd_h[...] = jnp.zeros_like(bd_h)
    bd_l[...] = jnp.zeros_like(bd_l)
    lower = lax.broadcasted_iota(jnp.int32, (CHUNK, CHUNK), 0) >= lax.broadcasted_iota(
        jnp.int32, (CHUNK, CHUNK), 1
    )

    loads[0].wait()
    kh[...], kl[...] = split(k_s[...])
    loads[1].wait()
    vh[...], vl[...] = split(v_s[...])
    total = jnp.zeros((heads * HD, HD), F32)
    for c in range(chunks):
        here = diagonal(dot3(pair(kh, kl, rows(c)), pair(vh, vl, rows(c)), TN))
        total = total + here
        if c + 1 < chunks:
            put_block_diagonal(c, total)
    own[0] = total
    pl.semaphore_wait(barrier, len(peers))
    relay_signal(col_sem, n_y, col_peer, 0)
    relay_signal(head_sem, n_head, head_peer, 0)
    scan_row(0)

    loads[2].wait()
    qh[...], ql[...] = split(q_s[...])
    for c in range(chunks):
        for i in range(heads):
            scores = dot3(
                pair(qh, ql, rows(c), cols(i)), pair(kh, kl, rows(c), cols(i)), NT
            )
            sco_h[c, i], sco_l[c, i] = split(jnp.where(lower, scores, 0.0))
        if c == 0:
            relay_wait(col_sem, n_y, 0)
            relay_signal(col_sem, n_y, col_peer, 1)
            relay_wait(head_sem, n_head, 0)
            relay_signal(head_sem, n_head, head_peer, 1)
    loads[3].wait()
    loads[4].wait()
    sc_s[...] = sc_s[...] * gain_s[...]
    scan_col(0)
    relay_wait(head_sem, n_head, 1)
    relay_signal(head_sem, n_head, head_peer, 2)
    scan_within(0)
    qt_h[...], qt_l[...] = split(q_s[...].T)
    for c in range(chunks):
        for i in range(heads):
            inner = dot3(pair(sco_h, sco_l, c, i), pair(vh, vl, rows(c), cols(i)), NN)
            att_s[rows(c), cols(i)] = inner
        if c > 0:
            att_s[rows(c)] += dot3(
                pair(qh, ql, rows(c)), pair(bd_h, bd_l, c - 1), NN
            )
    scan_back(0)
    scan_end(0)

    put_block_diagonal(chunks, state[0])
    lane = lax.broadcasted_iota(jnp.int32, (HD, HD), 1)
    groups = tokens // HD
    sums = jnp.zeros((HD, HD), F32)
    before = pair(bd_h, bd_l, chunks)
    for g in range(groups):
        piece = slice(g * HD, (g + 1) * HD)
        att = att_s[piece] + dot3(pair(qh, ql, piece), before, NN)
        att_s[piece] = att
        squares = jnp.sum(att * att, axis=1, keepdims=True)
        cross = jnp.sum(att * sc_s[piece], axis=1, keepdims=True)
        sums = jnp.where(lane == g, squares, sums)
        sums = jnp.where(lane == groups + g, cross, sums)
    norm_own[...] = sums.T[: 2 * groups]
    relay_wait(head_sem, n_head, 2)
    for m in far_first(n_head):
        send(norm_own, norm_in.at[m - 1], 4, head_peer(m))
    both = norm_own[...]
    if n_head > 1:
        wait_in(norm_in, 4)
        for m in range(1, n_head):
            both = both + norm_in[m - 1]
    mean = both / (width * n_head)
    inverse = lax.rsqrt(mean[:groups] + EPS)
    slope = inverse * inverse * inverse * mean[groups:]
    factors = jnp.concatenate(
        [inverse, slope, jnp.zeros((HD - 2 * groups, HD), F32)], axis=0
    ).T
    for g in range(groups):
        piece = slice(g * HD, (g + 1) * HD)
        grad = (
            factors[:, g : g + 1] * sc_s[piece]
            - factors[:, groups + g : groups + g + 1] * att_s[piece]
        )
        gh[piece], gl[piece] = split(grad)

    total = jnp.zeros((heads * HD, HD), F32)
    for c in reversed(range(chunks)):
        here = diagonal(
            dot3((qt_h[:, rows(c)], qt_l[:, rows(c)]), pair(gh, gl, rows(c)), NN)
        )
        total = total + here
        if c > 0:
            put_block_diagonal(chunks + c, total)
    own[1] = total
    scan_row(1)

    def mix(c):
        for i in range(heads):
            here = (rows(c), cols(i))
            mixing = dot3(pair(gh, gl, *here), pair(vh, vl, *here), NT)
            mixing = split(jnp.where(lower, mixing, 0.0))
            gq_s[here] = dot3(mixing, pair(kh, kl, *here), NN)
            gk_s[here] = dot3(mixing, pair(qh, ql, *here), TN)
            gv_s[here] = dot3(pair(sco_h, sco_l, c, i), pair(gh, gl, *here), TN)
        gq_s[rows(c)] += dot3(pair(gh, gl, rows(c)), pair(bd_h, bd_l, chunks), NT)
        if c > 0:
            gq_s[rows(c)] += dot3(pair(gh, gl, rows(c)), pair(bd_h, bd_l, c - 1), NT)
        if c + 1 < chunks:
            after = pair(bd_h, bd_l, chunks + c + 1)
            gk_s[rows(c)] += dot3(pair(vh, vl, rows(c)), after, NT)
            gv_s[rows(c)] += dot3(pair(kh, kl, rows(c)), after, NN)

    mix(0)
    scan_col(1)
    scan_within(1)
    for c in range(1, chunks):
        mix(c)
    sent(0)
    wait_out(row_out.at[0, pl.ds(1, ROW - 1)], 1)
    if n_head > 1:
        wait_out(norm_in, 4)
    after_h[...] = jnp.zeros_like(after_h)
    after_l[...] = jnp.zeros_like(after_l)
    scan_back(1)
    sent(1)
    scan_end(1)

    high, low = split(state[1])
    for i in range(heads):
        after_h[cols(i), cols(i)] = high[cols(i)]
        after_l[cols(i), cols(i)] = low[cols(i)]
    wait_out(row_out.at[1, pl.ds(1, ROW - 1)], 3)


def finish(
    gq_s, gk_s, gv_s, kh, kl, vh, vl, after_h, after_l, gq_hbm, gk_hbm, gv_hbm, k_out, v_out, sem
):
    after = (after_h[...], after_l[...])
    stores = [pltpu.make_async_copy(gq_s, gq_hbm, sem.at[0])]
    stores[0].start()

    def store(src, dst, piece):
        stores.append(pltpu.make_async_copy(src.at[piece], dst.at[piece], sem.at[len(stores)]))
        stores[-1].start()

    for c in range(gq_s.shape[0] // CHUNK):
        piece = pl.ds(c * CHUNK, CHUNK)
        k_out[piece] = gk_s[piece] + dot3((vh[piece], vl[piece]), after, NT)
        store(k_out, gk_hbm, piece)
        v_out[piece] = gv_s[piece] + dot3((kh[piece], kl[piece]), after, NN)
        store(v_out, gv_hbm, piece)
    for copy in stores:
        copy.wait()


def shards(n_seq, n_head, queries, keys, values, cotangent, gain):
    tokens, width = queries.shape
    heads = width // HD
    chunks = tokens // CHUNK
    n_y = n_seq // ROW
    part = heads * HD // ROW
    full = (tokens, width)
    norm_rows = 2 * tokens // HD
    anywhere = pl.BlockSpec(memory_space=pl.ANY)
    vmem = pl.BlockSpec(memory_space=pltpu.VMEM)
    blocks = pl.pallas_call(
        functools.partial(body, n_seq, n_head),
        out_shape=(pltpu.VMEM(full, F32),) * 3
        + (pltpu.VMEM(full, BF16),) * 4
        + (pltpu.VMEM((width, width), BF16),) * 2,
        in_specs=[anywhere] * 5,
        out_specs=(vmem,) * 9,
        scratch_shapes=[pltpu.VMEM(full, F32)] * 4
        + [pltpu.VMEM((1, width), F32), pltpu.VMEM(full, F32)]
        + [pltpu.VMEM(full, BF16)] * 4
        + [pltpu.VMEM((width, tokens), BF16)] * 2
        + [pltpu.VMEM((chunks, heads, CHUNK, CHUNK), BF16)] * 2
        + [pltpu.VMEM((2 * chunks, width, width), BF16)] * 2
        + [
            pltpu.VMEM((2, heads * HD, HD), F32),
            pltpu.VMEM((2, ROW - 1, part, HD), F32),
            pltpu.VMEM((2, n_y, part, HD), F32),
            pltpu.VMEM((2, ROW, part, HD), F32),
            pltpu.VMEM((2, heads * HD, HD), F32),
            pltpu.VMEM((norm_rows, HD), F32),
            pltpu.VMEM((max(n_head - 1, 1), norm_rows, HD), F32),
            pltpu.SemaphoreType.DMA((5,)),
            pltpu.SemaphoreType.DMA((5,)),
            pltpu.SemaphoreType.DMA((5,)),
            pltpu.SemaphoreType.DMA((2, max(n_y - 1, 1))),
            pltpu.SemaphoreType.DMA((2, max(n_y - 1, 1))),
            pltpu.SemaphoreType.REGULAR((3,)),
            pltpu.SemaphoreType.REGULAR((3,)),
        ],
        compiler_params=pltpu.CompilerParams(collective_id=0, has_side_effects=True),
    )(queries, keys, values, cotangent, gain[None, :])
    out = jax.ShapeDtypeStruct(full, F32)
    return tuple(
        pl.pallas_call(
            finish,
            out_shape=(out, out, out),
            in_specs=[vmem] * 9,
            out_specs=(anywhere,) * 3,
            scratch_shapes=[pltpu.VMEM(full, F32)] * 2 + [pltpu.SemaphoreType.DMA((1 + 2 * chunks,))],
        )(*(pltpu.with_memory_space_constraint(b, pltpu.VMEM) for b in blocks))
    )


def solution(mesh):
    in_specs = (P("seq", "head"), P("seq", "head"), P("seq", "head"), P("seq", "head"), P("head"))
    out_specs = (P("seq", "head"), P("seq", "head"), P("seq", "head"))
    return jax.shard_map(
        functools.partial(shards, mesh.shape["seq"], mesh.shape["head"]),
        mesh=mesh,
        in_specs=in_specs,
        out_specs=out_specs,
        check_vma=False,
    )
```

```python
import functools

import jax
import jax.numpy as jnp
from jax import lax
from jax.experimental import pallas as pl
from jax.experimental.pallas import tpu as pltpu
from jax.sharding import PartitionSpec as P

HD = 128
ROW = 8
CHUNK = 256
EPS = 1e-06
MESH = pl.DeviceIdType.MESH
F32 = jnp.float32
BF16 = jnp.bfloat16


def split(x):
    high = x.astype(BF16)
    return high, (x - high.astype(F32)).astype(BF16)


def dot3(left, right, dims):
    (lh, ll), (rh, rl) = left, right
    (lc,), (rc,) = dims
    return lax.dot_general(
        jnp.concatenate([lh, lh, ll], axis=lc),
        jnp.concatenate([rh, rl, rh], axis=rc),
        (dims, ((), ())),
        preferred_element_type=F32,
    )


def far_first(count):
    return sorted(range(1, count), key=lambda m: -min(m, count - m))


def row_order(count):
    return sorted(range(1, count), key=lambda k: -(min(k, count - k) + 1.5 * (k % 2)))


def relay_steps(count):
    known, steps = 1, []
    while 2 * known + 1 < count:
        step = min(known, count // 2 - known)
        steps.append(step)
        known += step
    return steps


NN = ((1,), (0,))
NT = ((1,), (1,))
TN = ((0,), (0,))


def body(
    n_seq,
    n_head,
    q_hbm,
    k_hbm,
    v_hbm,
    cot_hbm,
    gain_hbm,
    gq_s,
    gk_s,
    gv_s,
    kh,
    kl,
    vh,
    vl,
    after_h,
    after_l,
    q_s,
    k_s,
    v_s,
    sc_s,
    gain_s,
    att_s,
    qh,
    ql,
    gh,
    gl,
    qt_h,
    qt_l,
    sco_h,
    sco_l,
    bd_h,
    bd_l,
    own,
    row_in,
    col_in,
    row_out,
    state,
    norm_own,
    norm_in,
    in_sem,
    send_sem,
    recv_sem,
    col_send,
    col_recv,
    col_sem,
    head_sem,
):
    n_y = n_seq // ROW
    tokens, width = q_s.shape
    heads = width // HD
    chunks = tokens // CHUNK
    part = heads * HD // ROW
    s = lax.axis_index("seq")
    h = lax.axis_index("head")
    j = lax.rem(s, ROW)
    y = lax.div(s, ROW)

    def row_peer(k):
        return (y * ROW + lax.rem(j + k, ROW), h)

    def col_peer(m):
        return (lax.rem(y + m, n_y) * ROW + j, h)

    def head_peer(m):
        return (s, lax.rem(h + m, n_head))

    def near(count, peer):
        return [peer(m) for m in sorted({1, count - 1}) if 0 < m < count]

    barrier = pltpu.get_barrier_semaphore()
    peers = (
        [row_peer(k) for k in row_order(ROW)] + near(n_y, col_peer) + near(n_head, head_peer)
    )
    for peer in peers:
        pl.semaphore_signal(barrier, inc=1, device_id=peer, device_id_type=MESH)
    loads = [
        pltpu.make_async_copy(src, dst, in_sem.at[i])
        for i, (src, dst) in enumerate(
            [(k_hbm, k_s), (v_hbm, v_s), (q_hbm, q_s), (cot_hbm, sc_s), (gain_hbm, gain_s)]
        )
    ]
    for load in loads:
        load.start()

    def relay_signal(sem, count, peer, number):
        steps = relay_steps(count)
        if number < len(steps):
            for m in (steps[number], count - steps[number]):
                pl.semaphore_signal(
                    sem.at[number], inc=1, device_id=peer(m), device_id_type=MESH
                )

    def relay_wait(sem, count, number):
        if number < len(relay_steps(count)):
            pl.semaphore_wait(sem.at[number], 2)

    def remote(src, dst, sems, peer):
        return pltpu.make_async_remote_copy(
            src_ref=src,
            dst_ref=dst,
            send_sem=sems[0],
            recv_sem=sems[1],
            device_id=peer,
            device_id_type=MESH,
        )

    def sems(stage):
        return send_sem.at[stage], recv_sem.at[stage]

    def send(src, dst, stage, peer):
        remote(src, dst, sems(stage), peer).start()

    def wait_in(ref, stage):
        remote(ref, ref, sems(stage), row_peer(1)).wait_recv()

    def wait_out(ref, stage):
        remote(ref, ref, sems(stage), row_peer(1)).wait_send()

    def col_copy(scan, m):
        return remote(
            col_in.at[scan, n_y - 1],
            col_in.at[scan, m - 1],
            (col_send.at[scan, m - 1], col_recv.at[scan, m - 1]),
            col_peer(m),
        )

    def goes(scan, m):
        return (y + m >= n_y) if scan else (y + m < n_y)

    def comes(scan, m):
        return (y < m) if scan else (y >= m)

    def weight(cond):
        return jnp.where(cond, 1.0, 0.0).astype(F32)

    def scan_row(scan):
        for k in row_order(ROW):
            there = lax.rem(j + k, ROW)
            send(
                own.at[scan, pl.ds(pl.multiple_of(there * part, part), part)],
                row_in.at[scan, k - 1],
                2 * scan,
                row_peer(k),
            )

    def scan_col(scan):
        wait_in(row_in.at[scan], 2 * scan)
        total = own[scan, pl.ds(pl.multiple_of(j * part, part), part)]
        for k in range(1, ROW):
            total = total + row_in[scan, k - 1]
        col_in[scan, n_y - 1] = total
        if scan == 0:
            relay_wait(col_sem, n_y, 1)
        for m in far_first(n_y):

            @pl.when(goes(scan, m))
            def _():
                col_copy(scan, m).start()

    def scan_within(scan):
        for k in row_order(ROW) + [0]:
            there = lax.rem(j + k, ROW)
            value = jnp.zeros((part, HD), F32)
            for r in range(ROW):
                source = lax.rem(j - r + ROW, ROW)
                inside = (source > there) if scan else (source < there)
                piece = (
                    row_in[scan, r - 1]
                    if r
                    else own[scan, pl.ds(pl.multiple_of(j * part, part), part)]
                )
                value = value + weight(inside) * piece
            row_out[scan, k] = value

    def scan_back(scan):
        base = jnp.zeros((part, HD), F32)
        for m in reversed(far_first(n_y)):

            @pl.when(comes(scan, m))
            def _():
                col_copy(scan, m).wait_recv()

            base = base + jnp.where(comes(scan, m), col_in[scan, m - 1], 0.0)
        here = pl.ds(pl.multiple_of(j * part, part), part)
        for k in row_order(ROW):
            row_out[scan, k] += base
            send(row_out.at[scan, k], state.at[scan, here], 2 * scan + 1, row_peer(k))
        state[scan, here] = row_out[scan, 0] + base

    def sent(scan):
        wait_out(row_in.at[scan], 2 * scan)
        for m in range(1, n_y):

            @pl.when(goes(scan, m))
            def _():
                col_copy(scan, m).wait_send()

    def scan_end(scan):
        wait_in(state.at[scan, pl.ds(0, (ROW - 1) * part)], 2 * scan + 1)

    def cols(head):
        return slice(head * HD, (head + 1) * HD)

    def rows(chunk):
        return slice(chunk * CHUNK, (chunk + 1) * CHUNK)

    def diagonal(full):
        return jnp.concatenate([full[cols(i), cols(i)] for i in range(heads)], axis=0)

    def put_block_diagonal(slot, stacked):
        high, low = split(stacked)
        for i in range(heads):
            bd_h[slot, cols(i), cols(i)] = high[cols(i)]
            bd_l[slot, cols(i), cols(i)] = low[cols(i)]

    def pair(high, low, *index):
        return high[index], low[index]

    bd_h[...] = jnp.zeros_like(bd_h)
    bd_l[...] = jnp.zeros_like(bd_l)
    lower = lax.broadcasted_iota(jnp.int32, (CHUNK, CHUNK), 0) >= lax.broadcasted_iota(
        jnp.int32, (CHUNK, CHUNK), 1
    )

    loads[0].wait()
    kh[...], kl[...] = split(k_s[...])
    loads[1].wait()
    vh[...], vl[...] = split(v_s[...])
    total = jnp.zeros((heads * HD, HD), F32)
    for c in range(chunks):
        here = diagonal(dot3(pair(kh, kl, rows(c)), pair(vh, vl, rows(c)), TN))
        total = total + here
        if c + 1 < chunks:
            put_block_diagonal(c, total)
    own[0] = total
    pl.semaphore_wait(barrier, len(peers))
    relay_signal(col_sem, n_y, col_peer, 0)
    relay_signal(head_sem, n_head, head_peer, 0)
    scan_row(0)

    loads[2].wait()
    qh[...], ql[...] = split(q_s[...])
    for c in range(chunks):
        for i in range(heads):
            scores = dot3(
                pair(qh, ql, rows(c), cols(i)), pair(kh, kl, rows(c), cols(i)), NT
            )
            sco_h[c, i], sco_l[c, i] = split(jnp.where(lower, scores, 0.0))
        if c == 0:
            relay_wait(col_sem, n_y, 0)
            relay_signal(col_sem, n_y, col_peer, 1)
            relay_wait(head_sem, n_head, 0)
            relay_signal(head_sem, n_head, head_peer, 1)
    loads[3].wait()
    loads[4].wait()
    sc_s[...] = sc_s[...] * gain_s[...]
    scan_col(0)
    relay_wait(head_sem, n_head, 1)
    relay_signal(head_sem, n_head, head_peer, 2)
    scan_within(0)
    qt_h[...], qt_l[...] = split(q_s[...].T)
    for c in range(chunks):
        for i in range(heads):
            inner = dot3(pair(sco_h, sco_l, c, i), pair(vh, vl, rows(c), cols(i)), NN)
            att_s[rows(c), cols(i)] = inner
        if c > 0:
            att_s[rows(c)] += dot3(
                pair(qh, ql, rows(c)), pair(bd_h, bd_l, c - 1), NN
            )
    scan_back(0)
    scan_end(0)

    put_block_diagonal(chunks, state[0])
    lane = lax.broadcasted_iota(jnp.int32, (HD, HD), 1)
    groups = tokens // HD
    sums = jnp.zeros((HD, HD), F32)
    before = pair(bd_h, bd_l, chunks)
    for g in range(groups):
        piece = slice(g * HD, (g + 1) * HD)
        att = att_s[piece] + dot3(pair(qh, ql, piece), before, NN)
        att_s[piece] = att
        squares = jnp.sum(att * att, axis=1, keepdims=True)
        cross = jnp.sum(att * sc_s[piece], axis=1, keepdims=True)
        sums = jnp.where(lane == g, squares, sums)
        sums = jnp.where(lane == groups + g, cross, sums)
    norm_own[...] = sums.T[: 2 * groups]
    relay_wait(head_sem, n_head, 2)
    for m in far_first(n_head):
        send(norm_own, norm_in.at[m - 1], 4, head_peer(m))
    both = norm_own[...]
    if n_head > 1:
        wait_in(norm_in, 4)
        for m in range(1, n_head):
            both = both + norm_in[m - 1]
    mean = both / (width * n_head)
    inverse = lax.rsqrt(mean[:groups] + EPS)
    slope = inverse * inverse * inverse * mean[groups:]
    factors = jnp.concatenate(
        [inverse, slope, jnp.zeros((HD - 2 * groups, HD), F32)], axis=0
    ).T
    for g in range(groups):
        piece = slice(g * HD, (g + 1) * HD)
        grad = (
            factors[:, g : g + 1] * sc_s[piece]
            - factors[:, groups + g : groups + g + 1] * att_s[piece]
        )
        gh[piece], gl[piece] = split(grad)

    total = jnp.zeros((heads * HD, HD), F32)
    for c in reversed(range(chunks)):
        here = diagonal(
            dot3((qt_h[:, rows(c)], qt_l[:, rows(c)]), pair(gh, gl, rows(c)), NN)
        )
        total = total + here
        if c > 0:
            put_block_diagonal(chunks + c, total)
    own[1] = total
    scan_row(1)

    def mix(c):
        for i in range(heads):
            here = (rows(c), cols(i))
            mixing = dot3(pair(gh, gl, *here), pair(vh, vl, *here), NT)
            mixing = split(jnp.where(lower, mixing, 0.0))
            gq_s[here] = dot3(mixing, pair(kh, kl, *here), NN)
            gk_s[here] = dot3(mixing, pair(qh, ql, *here), TN)
            gv_s[here] = dot3(pair(sco_h, sco_l, c, i), pair(gh, gl, *here), TN)
        gq_s[rows(c)] += dot3(pair(gh, gl, rows(c)), pair(bd_h, bd_l, chunks), NT)
        if c > 0:
            gq_s[rows(c)] += dot3(pair(gh, gl, rows(c)), pair(bd_h, bd_l, c - 1), NT)
        if c + 1 < chunks:
            after = pair(bd_h, bd_l, chunks + c + 1)
            gk_s[rows(c)] += dot3(pair(vh, vl, rows(c)), after, NT)
            gv_s[rows(c)] += dot3(pair(kh, kl, rows(c)), after, NN)

    mix(0)
    scan_col(1)
    scan_within(1)
    for c in range(1, chunks):
        mix(c)
    sent(0)
    wait_out(row_out.at[0, pl.ds(1, ROW - 1)], 1)
    if n_head > 1:
        wait_out(norm_in, 4)
    after_h[...] = jnp.zeros_like(after_h)
    after_l[...] = jnp.zeros_like(after_l)
    scan_back(1)
    sent(1)
    scan_end(1)

    high, low = split(state[1])
    for i in range(heads):
        after_h[cols(i), cols(i)] = high[cols(i)]
        after_l[cols(i), cols(i)] = low[cols(i)]
    wait_out(row_out.at[1, pl.ds(1, ROW - 1)], 3)


def finish(
    gq_s, gk_s, gv_s, kh, kl, vh, vl, after_h, after_l, gq_hbm, gk_hbm, gv_hbm, k_out, v_out, sem
):
    after = (after_h[...], after_l[...])
    stores = [pltpu.make_async_copy(gq_s, gq_hbm, sem.at[0])]
    stores[0].start()

    def store(src, dst, piece):
        stores.append(pltpu.make_async_copy(src.at[piece], dst.at[piece], sem.at[len(stores)]))
        stores[-1].start()

    for c in range(gq_s.shape[0] // CHUNK):
        piece = pl.ds(c * CHUNK, CHUNK)
        k_out[piece] = gk_s[piece] + dot3((vh[piece], vl[piece]), after, NT)
        store(k_out, gk_hbm, piece)
        v_out[piece] = gv_s[piece] + dot3((kh[piece], kl[piece]), after, NN)
        store(v_out, gv_hbm, piece)
    for copy in stores:
        copy.wait()


def shards(n_seq, n_head, queries, keys, values, cotangent, gain):
    tokens, width = queries.shape
    heads = width // HD
    chunks = tokens // CHUNK
    n_y = n_seq // ROW
    part = heads * HD // ROW
    full = (tokens, width)
    norm_rows = 2 * tokens // HD
    anywhere = pl.BlockSpec(memory_space=pl.ANY)
    vmem = pl.BlockSpec(memory_space=pltpu.VMEM)
    blocks = pl.pallas_call(
        functools.partial(body, n_seq, n_head),
        out_shape=(pltpu.VMEM(full, F32),) * 3
        + (pltpu.VMEM(full, BF16),) * 4
        + (pltpu.VMEM((width, width), BF16),) * 2,
        in_specs=[anywhere] * 5,
        out_specs=(vmem,) * 9,
        scratch_shapes=[pltpu.VMEM(full, F32)] * 4
        + [pltpu.VMEM((1, width), F32), pltpu.VMEM(full, F32)]
        + [pltpu.VMEM(full, BF16)] * 4
        + [pltpu.VMEM((width, tokens), BF16)] * 2
        + [pltpu.VMEM((chunks, heads, CHUNK, CHUNK), BF16)] * 2
        + [pltpu.VMEM((2 * chunks, width, width), BF16)] * 2
        + [
            pltpu.VMEM((2, heads * HD, HD), F32),
            pltpu.VMEM((2, ROW - 1, part, HD), F32),
            pltpu.VMEM((2, n_y, part, HD), F32),
            pltpu.VMEM((2, ROW, part, HD), F32),
            pltpu.VMEM((2, heads * HD, HD), F32),
            pltpu.VMEM((norm_rows, HD), F32),
            pltpu.VMEM((max(n_head - 1, 1), norm_rows, HD), F32),
            pltpu.SemaphoreType.DMA((5,)),
            pltpu.SemaphoreType.DMA((5,)),
            pltpu.SemaphoreType.DMA((5,)),
            pltpu.SemaphoreType.DMA((2, max(n_y - 1, 1))),
            pltpu.SemaphoreType.DMA((2, max(n_y - 1, 1))),
            pltpu.SemaphoreType.REGULAR((3,)),
            pltpu.SemaphoreType.REGULAR((3,)),
        ],
        compiler_params=pltpu.CompilerParams(collective_id=0, has_side_effects=True),
    )(queries, keys, values, cotangent, gain[None, :])
    out = jax.ShapeDtypeStruct(full, F32)
    return tuple(
        pl.pallas_call(
            finish,
            out_shape=(out, out, out),
            in_specs=[vmem] * 9,
            out_specs=(anywhere,) * 3,
            scratch_shapes=[pltpu.VMEM(full, F32)] * 2 + [pltpu.SemaphoreType.DMA((1 + 2 * chunks,))],
        )(*(pltpu.with_memory_space_constraint(b, pltpu.VMEM) for b in blocks))
    )


def solution(mesh):
    in_specs = (P("seq", "head"), P("seq", "head"), P("seq", "head"), P("seq", "head"), P("head"))
    out_specs = (P("seq", "head"), P("seq", "head"), P("seq", "head"))
    return jax.shard_map(
        functools.partial(shards, mesh.shape["seq"], mesh.shape["head"]),
        mesh=mesh,
        in_specs=in_specs,
        out_specs=out_specs,
        check_vma=False,
    )
```
